256 devices in a mesh: dp: 2 (over y_lo), vocab: 128 (over z, x, y_hi, core).
Axes of the slice: x: 4, y: 4 (y_hi: 2, y_lo: 2; y = y_hi * 2 + y_lo), z: 8, core: 2. Of those that a mesh axis runs over, the one named last changes fastest.
Arguments:
- token_ids: int32 [1024], P(('dp', 'vocab')), may hold values from 0 to 131071
- hidden: bfloat16 [1024, 2304], P(('dp', 'vocab')), may hold values from -6 to 6
- logit_grad: bfloat16 [1024, 131072], P('dp', 'vocab'), may hold values from -0.1875 to 0.1875
- embed_grad: bfloat16 [1024, 2304], P(('dp', 'vocab')), may hold values from -6 to 6
Outputs:
- weight_grad: float32 [131072, 2304], P('vocab', 'dp')
The draws below stay inside these ranges and needn't reach their ends.
All inputs are finite; a program needn't handle non-finite values.
Results may differ from the reference program's by a relative error of at most 0.0003.
Values may be sent and summed in bfloat16 or wider, within the bound.
No kernel may reach another device: no remote copies, remote signals or barrier semaphores. Data moves between devices by JAX's collectives and lax.ppermute only.
A program may use at most 64 MiB of HBM per device.

```python
import math
import jax
import jax.numpy as jnp
import numpy as np
from jax import lax

D = 2304
V = 131072
TOKENS = 1024


def set_ends(values, key, low, high):
    longest = values.shape.index(max(values.shape))
    spots = []
    for shift in (0, 1):
        where = [jax.random.randint(jax.random.fold_in(key, axis), (), 0, length) for axis, length in enumerate(values.shape)]
        where[longest] = (where[longest] + shift) % values.shape[longest]
        spots.append(tuple(where))
    return values.at[spots[0]].set(low).at[spots[1]].set(high)


def levels(stream_key, shape, pieces, smallest, high):
    def one(axis_at, blocks):
        draws = jax.random.uniform(jax.random.fold_in(jax.random.fold_in(stream_key, 6), axis_at), (blocks,), jnp.float32, smallest / len(pieces), high / len(pieces))
        return jnp.repeat(jnp.exp(draws), shape[axis_at] // blocks).reshape((-1,) + (1,) * (len(shape) - axis_at - 1))

    level = one(*pieces[0])
    for cut in pieces[1:]:
        level = level * one(*cut)
    return level


def wide_ids(rng, shape, amount, slope):
    weights = [min(1 << octave, amount + 1 - (1 << octave)) * (1 << 20) // math.isqrt((1 << octave) ** slope) + 1 for octave in range((amount + 1).bit_length()) if 1 << octave <= amount]
    deviation = 1 + sum(weights) // (1 << 30)
    listing = np.cumsum(np.array([max(1, weight // deviation) for weight in weights]))
    pick = jax.random.randint(jax.random.fold_in(rng, 1), shape, 0, int(listing[len(weights) - 1]))
    start = jnp.left_shift(1, jnp.searchsorted(jnp.asarray(listing, jnp.int32), pick, side="right").astype(jnp.int32))
    rank = start - 1 + jax.random.randint(jax.random.fold_in(rng, 4), shape, 0, 1 << 30) % jnp.minimum(start, amount + 1 - start)
    return jax.random.permutation(jax.random.fold_in(rng, 2), amount)[rank].astype(jnp.int32)


def bell_draw(key, extent, width, limit, cuts=(), kind=jnp.bfloat16):
    values = width * jax.random.normal(key, extent, jnp.float32)
    if cuts:
        values = values * levels(key, extent, cuts, -0.22, 0.18)
    return jnp.clip(values, -limit, limit).astype(kind)


def setup_inputs(seed: int = 0) -> dict:
    key_list = jax.random.split(jax.random.key(seed), 5)
    return {
        "token_ids": set_ends(wide_ids(key_list[0], (TOKENS,), V, 2), jax.random.fold_in(key_list[0], 3), 0, V - 1).astype(jnp.int32),
        "hidden": bell_draw(key_list[1], (TOKENS, D), 1.0, 6.0, ((0, 256),)),
        "logit_grad": bell_draw(key_list[2], (TOKENS, V), (TOKENS ** -0.5), 0.1875, ((0, 2), (1, 128))),
        "embed_grad": bell_draw(key_list[3], (TOKENS, D), 1.0, 6.0, ((0, 256),)),
    }


def reference(token_ids, hidden, logit_grad, embed_grad):
    output_side = lax.dot_general(logit_grad, hidden, (((0,), (0,)), ((), ())), preferred_element_type=jnp.float32)
    input_side = jax.ops.segment_sum(embed_grad.astype(jnp.float32), token_ids.astype(jnp.int32), num_segments=V)
    return output_side + input_side
```

```python
import functools

import jax
import jax.numpy as jnp
import numpy as np
from jax import lax
from jax.experimental import pallas as pl
from jax.experimental.pallas import tpu as pltpu
from jax.sharding import PartitionSpec as P

Z, X, YH, CORE, DP = 8, 4, 2, 2, 2
ROWS = 4
LANES = 128


def coords(vocab):
    return vocab // (X * 4), (vocab // 4) % X, (vocab // 2) % 2, vocab % 2


def flat(dp, z, x, yh, core):
    return dp * (Z * X * 4) + ((z % Z) * X + (x % X)) * 4 + yh * 2 + core


def move(value, dz=0, dx=0, fy=0, fd=0, fc=0):
    pairs = []
    for dp in range(DP):
        for vocab in range(Z * X * 4):
            z, x, yh, core = coords(vocab)
            pairs.append((flat(dp, z, x, yh, core), flat(dp ^ fd, z + dz, x + dx, yh ^ fy, core ^ fc)))
    return lax.ppermute(value, ("dp", "vocab"), pairs)


def gather_tokens(own, other):
    from_dp = move(other, fd=1)
    from_dy = move(other, fd=1, fy=1)
    from_yh = move(own, fy=1)
    chunk = jnp.concatenate([own, from_dp, from_yh, from_dy], axis=0)
    right, left, ups, downs = chunk, chunk, [], []
    for step in range(Z // 2):
        right = move(right, dz=1)
        downs.append(right)
        if step < Z // 2 - 1:
            left = move(left, dz=-1)
            ups.append(left)
    column = jnp.concatenate([chunk] + ups + downs[::-1], axis=0)
    down = move(column, dx=1)
    up = move(column, dx=-1)
    half = column.shape[0] // 2
    across = jnp.concatenate([move(down[:half], dx=1), move(up[half:], dx=-1)], axis=0)
    mine = [column, up, across, down]
    return mine + [move(part, fc=1) for part in mine], from_yh


def arrangement(dp, vocab):
    z, x, yh, core = coords(vocab)
    place = lax.broadcasted_iota(jnp.int32, (1, 2 * Z * X * YH * CORE * ROWS), 1)
    j, r, zi = place % 4, (place // 4) % 4, (place // 16) % Z
    xi, ci = (place // (16 * Z)) % X, place // (16 * Z * X)
    token = ((((z + zi) % Z) * X + (x + xi) % X) * 2 + (yh ^ (r // 2))) * 2 + (core ^ ci)
    token = token * ROWS + j
    spot = lax.broadcasted_iota(jnp.int32, (Z * X * YH * CORE * ROWS, 1), 0)
    hit = spot == token
    near = r % 2 == 0
    return (hit & near).astype(jnp.bfloat16), (hit & ~near).astype(jnp.bfloat16)


def contract_kernel(parts, offset_ref, logit_ref, *refs):
    features = refs[:parts]
    grads = refs[parts : 2 * parts]
    codes = refs[2 * parts : 3 * parts]
    out_ref, onehot = refs[3 * parts :]
    rows, length = logit_ref.shape[0], features[0].shape[0]

    @pl.when(pl.program_id(0) == 0)
    def _():
        lane = lax.broadcasted_iota(jnp.int32, (8, LANES), 1)
        weight = jnp.where(lane == 0, 512.0, jnp.where(lane == 1, 2.0, jnp.where(lane == 2, 1.0, 0.0)))
        weight = weight.astype(jnp.bfloat16)
        row = lax.broadcasted_iota(jnp.int32, (rows, length), 0) + offset_ref[0]
        for k in range(parts):
            ids = lax.dot_general(
                weight, codes[k][...], (((1,), (1,)), ((), ())), preferred_element_type=jnp.float32
            )[:1].astype(jnp.int32)
            onehot[:, k * length : (k + 1) * length] = jnp.where(row == ids, 1.0, 0.0).astype(jnp.bfloat16)

    step = 256

    @pl.loop(0, rows // step)
    def _(block):
        span = pl.ds(pl.multiple_of(block * step, step), step)
        right = jnp.concatenate([f[...] for f in features], axis=0)
        total = jnp.dot(logit_ref[span, :], right, preferred_element_type=jnp.float32)
        right = jnp.concatenate([g[...] for g in grads], axis=0)
        total += jnp.dot(onehot[span, :], right, preferred_element_type=jnp.float32)
        out_ref[span, :] = total


def contract(offset, logits, chunks, columns):
    parts = len(chunks)
    length = chunks[0].shape[0]
    rows, tokens = logits.shape
    width = 384
    steps = columns // width
    once = pl.Buffered(1)
    return pl.pallas_call(
        functools.partial(contract_kernel, parts),
        out_shape=jax.ShapeDtypeStruct((rows, columns), jnp.float32),
        grid=(steps,),
        in_specs=[
            pl.BlockSpec(memory_space=pltpu.SMEM),
            pl.BlockSpec((rows, tokens), lambda n: (0, 0), pipeline_mode=once),
        ]
        + [pl.BlockSpec((length, width), lambda n: (0, n))] * parts
        + [pl.BlockSpec((length, width), lambda n: (0, n + steps))] * parts
        + [pl.BlockSpec((length, LANES), lambda n: (0, 2 * columns // LANES), pipeline_mode=once)] * parts,
        out_specs=pl.BlockSpec((rows, width), lambda n: (0, n)),
        scratch_shapes=[pltpu.VMEM((rows, tokens), jnp.bfloat16)],
        compiler_params=pltpu.CompilerParams(vmem_limit_bytes=40 << 20),
        cost_estimate=pl.CostEstimate(
            flops=4 * rows * tokens * columns, bytes_accessed=12 << 20, transcendentals=0
        ),
    )(offset, logits, *chunks, *chunks, *chunks)


def body(token_ids, hidden, logit_grad, embed_grad):
    dp, vocab = lax.axis_index("dp"), lax.axis_index("vocab")
    columns = hidden.shape[1] // 2
    offset = (vocab * logit_grad.shape[1]).astype(jnp.int32).reshape(1)
    ids = token_ids[:, None]
    lane = lax.broadcasted_iota(jnp.int32, (ROWS, LANES), 1)
    code = jnp.where(lane == 0, ids // 512, jnp.where(lane == 1, (ids // 2) % 256, ids % 2))
    code = jnp.where(lane < 3, code, 0).astype(jnp.bfloat16)

    def payload(side):
        pick = [lax.dynamic_slice_in_dim(a, side * columns, columns, 1) for a in (hidden, embed_grad)]
        return jnp.concatenate(pick + [code], axis=1)

    near, far = arrangement(dp, vocab)
    dims = (((0,), (0,)), ((), ()))
    turned = lax.dot_general(logit_grad, near, dims, preferred_element_type=jnp.float32)
    chunks, early = gather_tokens(payload(dp), payload(1 - dp))
    held, _ = lax.optimization_barrier((logit_grad, early))
    partner = move(held, fd=1)
    turned = turned + lax.dot_general(partner, far, dims, preferred_element_type=jnp.float32)
    return contract(offset, turned.astype(jnp.bfloat16), chunks, columns)


def solution(mesh):
    placed = (
        P(("dp", "vocab")),
        P(("dp", "vocab"), None),
        P("dp", "vocab"),
        P(("dp", "vocab"), None),
    )
    return jax.shard_map(
        body, mesh=mesh, in_specs=placed, out_specs=P("vocab", "dp"), check_vma=False
    )
```

```python
import functools

import jax
import jax.numpy as jnp
import numpy as np
from jax import lax
from jax.experimental import pallas as pl
from jax.experimental.pallas import tpu as pltpu
from jax.sharding import PartitionSpec as P

Z, X, YH, CORE, DP = 8, 4, 2, 2, 2
ROWS = 4
LANES = 128


def coords(vocab):
    return vocab // (X * 4), (vocab // 4) % X, (vocab // 2) % 2, vocab % 2


def flat(dp, z, x, yh, core):
    return dp * (Z * X * 4) + ((z % Z) * X + (x % X)) * 4 + yh * 2 + core


def move(value, dz=0, dx=0, fy=0, fd=0, fc=0):
    pairs = []
    for dp in range(DP):
        for vocab in range(Z * X * 4):
            z, x, yh, core = coords(vocab)
            pairs.append((flat(dp, z, x, yh, core), flat(dp ^ fd, z + dz, x + dx, yh ^ fy, core ^ fc)))
    return lax.ppermute(value, ("dp", "vocab"), pairs)


def gather_column(own, other):
    from_dp = move(other, fd=1)
    from_dy = move(other, fd=1, fy=1)
    from_yh = move(own, fy=1)
    chunk = jnp.concatenate([own, from_dp, from_yh, from_dy], axis=0)
    right, left, ups, downs = chunk, chunk, [], []
    for step in range(Z // 2):
        right = move(right, dz=1)
        downs.append(right)
        if step < Z // 2 - 1:
            left = move(left, dz=-1)
            ups.append(left)
    return jnp.concatenate([chunk] + ups + downs[::-1], axis=0), from_yh


def arrangement(dp, vocab):
    z, x, yh, core = coords(vocab)
    place = lax.broadcasted_iota(jnp.int32, (1, 2 * Z * X * YH * CORE * ROWS), 1)
    j, r, zi = place % 4, (place // 4) % 4, (place // 16) % Z
    xi, ci = (place // (16 * Z)) % X, place // (16 * Z * X)
    token = ((((z + zi) % Z) * X + (x + xi) % X) * 2 + (yh ^ (r // 2))) * 2 + (core ^ ci)
    token = token * ROWS + j
    spot = lax.broadcasted_iota(jnp.int32, (Z * X * YH * CORE * ROWS, 1), 0)
    hit = spot == token
    near = r % 2 == 0
    return (hit & near).astype(jnp.bfloat16), (hit & ~near).astype(jnp.bfloat16)


def contract_kernel(spots, added, offset_ref, logit_ref, *refs):
    parts = len(spots)
    chunks = refs[:parts]
    out_ref, onehot = refs[parts + added :]
    rows, columns = out_ref.shape
    length = chunks[0].shape[0]
    lane = lax.broadcasted_iota(jnp.int32, (8, LANES), 1)
    weight = jnp.where(lane == 0, 512.0, jnp.where(lane == 1, 2.0, jnp.where(lane == 2, 1.0, 0.0)))
    weight = weight.astype(jnp.bfloat16)
    row = lax.broadcasted_iota(jnp.int32, (rows, length), 0) + (offset_ref[0] + pl.program_id(0) * rows)
    for k, chunk in enumerate(chunks):
        ids = lax.dot_general(
            weight, chunk[:, 2 * columns :], (((1,), (1,)), ((), ())), preferred_element_type=jnp.float32
        )[:1].astype(jnp.int32)
        onehot[:, k * length : (k + 1) * length] = jnp.where(row == ids, 1.0, 0.0).astype(jnp.bfloat16)
    left = jnp.concatenate([logit_ref[:, s * length : (s + 1) * length] for s in spots], axis=1)
    right = jnp.concatenate([c[:, :columns] for c in chunks], axis=0)
    total = jnp.dot(left, right, preferred_element_type=jnp.float32)
    right = jnp.concatenate([c[:, columns : 2 * columns] for c in chunks], axis=0)
    total += jnp.dot(onehot[...], right, preferred_element_type=jnp.float32)
    if added:
        total += refs[parts][...]
    out_ref[...] = total


def contract(offset, logits, chunks, spots, columns, partial=None):
    parts = len(chunks)
    length, width = chunks[0].shape
    rows, tokens = logits.shape
    block = 256
    added = [] if partial is None else [partial]
    return pl.pallas_call(
        functools.partial(contract_kernel, tuple(spots), len(added)),
        out_shape=jax.ShapeDtypeStruct((rows, columns), jnp.float32),
        grid=(rows // block,),
        in_specs=[
            pl.BlockSpec(memory_space=pltpu.SMEM),
            pl.BlockSpec((block, tokens), lambda m: (m, 0)),
        ]
        + [pl.BlockSpec((length, width), lambda m: (0, 0), pipeline_mode=pl.Buffered(1))] * parts
        + [pl.BlockSpec((block, columns), lambda m: (m, 0))] * len(added),
        out_specs=pl.BlockSpec((block, columns), lambda m: (m, 0)),
        scratch_shapes=[pltpu.VMEM((block, parts * length), jnp.bfloat16)],
        compiler_params=pltpu.CompilerParams(vmem_limit_bytes=28 << 20),
        cost_estimate=pl.CostEstimate(
            flops=4 * rows * parts * length * columns, bytes_accessed=12 << 20, transcendentals=0
        ),
    )(offset, logits, *chunks, *added)


def body(token_ids, hidden, logit_grad, embed_grad):
    dp, vocab = lax.axis_index("dp"), lax.axis_index("vocab")
    columns = hidden.shape[1] // 2
    offset = (vocab * logit_grad.shape[1]).astype(jnp.int32).reshape(1)
    ids = token_ids[:, None]
    lane = lax.broadcasted_iota(jnp.int32, (ROWS, LANES), 1)
    code = jnp.where(lane == 0, ids // 512, jnp.where(lane == 1, (ids // 2) % 256, ids % 2))
    code = jnp.where(lane < 3, code, 0).astype(jnp.bfloat16)

    def payload(side):
        pick = [lax.dynamic_slice_in_dim(a, side * columns, columns, 1) for a in (hidden, embed_grad)]
        return jnp.concatenate(pick + [code], axis=1)

    near, far = arrangement(dp, vocab)
    dims = (((0,), (0,)), ((), ()))
    column, early = gather_column(payload(dp), payload(1 - dp))
    held, _ = lax.optimization_barrier((logit_grad, early))
    partner = move(held, fd=1)
    down = move(column, dx=1)
    up = move(column, dx=-1)
    turned = lax.dot_general(logit_grad, near, dims, preferred_element_type=jnp.float32)
    turned = turned + lax.dot_general(partner, far, dims, preferred_element_type=jnp.float32)
    turned = turned.astype(jnp.bfloat16)
    down, up, turned = lax.optimization_barrier((down, up, turned))
    half = column.shape[0] // 2
    across = jnp.concatenate([move(down[:half], dx=1), move(up[half:], dx=-1)], axis=0)
    partial = contract(offset, turned, [column, up, down, move(column, fc=1)], (0, 1, 3, 4), columns)
    across, partial = lax.optimization_barrier((across, partial))
    rest = [across, move(up, fc=1), move(across, fc=1), move(down, fc=1)]
    return contract(offset, turned, rest, (2, 5, 6, 7), columns, partial)


def solution(mesh):
    placed = (
        P(("dp", "vocab")),
        P(("dp", "vocab"), None),
        P("dp", "vocab"),
        P(("dp", "vocab"), None),
    )
    return jax.shard_map(
        body, mesh=mesh, in_specs=placed, out_specs=P("vocab", "dp"), check_vma=False
    )
```

```python
import functools

import jax
import jax.numpy as jnp
import numpy as np
from jax import lax
from jax.experimental import pallas as pl
from jax.experimental.pallas import tpu as pltpu
from jax.sharding import PartitionSpec as P

Z, X, YH, CORE, DP = 8, 4, 2, 2, 2
ROWS = 4
LANES = 128


def coords(vocab):
    return vocab // (X * 4), (vocab // 4) % X, (vocab // 2) % 2, vocab % 2


def flat(dp, z, x, yh, core):
    return dp * (Z * X * 4) + ((z % Z) * X + (x % X)) * 4 + yh * 2 + core


def move(value, dz=0, dx=0, fy=0, fd=0, fc=0):
    pairs = []
    for dp in range(DP):
        for vocab in range(Z * X * 4):
            z, x, yh, core = coords(vocab)
            pairs.append((flat(dp, z, x, yh, core), flat(dp ^ fd, z + dz, x + dx, yh ^ fy, core ^ fc)))
    return lax.ppermute(value, ("dp", "vocab"), pairs)


def gather_column(own, other):
    from_dp = move(other, fd=1)
    from_dy = move(other, fd=1, fy=1)
    from_yh = move(own, fy=1)
    chunk = jnp.concatenate([own, from_dp, from_yh, from_dy], axis=0)
    p2, m2 = move(chunk, dz=2), move(chunk, dz=-2)
    p1, m1 = move(chunk, dz=1), move(chunk, dz=-1)
    p3, m3, m4 = move(p2, dz=1), move(m2, dz=-1), move(m2, dz=-2)
    return [chunk, m1, m2, m3], [m4, p3, p2, p1], from_yh


def arrangement(dp, vocab):
    z, x, yh, core = coords(vocab)
    place = lax.broadcasted_iota(jnp.int32, (1, 2 * Z * X * YH * CORE * ROWS), 1)
    j, r, zi = place % 4, (place // 4) % 4, (place // 16) % Z
    xi, ci = (place // (16 * Z)) % X, place // (16 * Z * X)
    token = ((((z + zi) % Z) * X + (x + xi) % X) * 2 + (yh ^ (r // 2))) * 2 + (core ^ ci)
    token = token * ROWS + j
    spot = lax.broadcasted_iota(jnp.int32, (Z * X * YH * CORE * ROWS, 1), 0)
    hit = spot == token
    near = r % 2 == 0
    return (hit & near).astype(jnp.bfloat16), (hit & ~near).astype(jnp.bfloat16)


def contract_kernel(spots, pieces, columns, added, last, offset_ref, logit_ref, *refs):
    chunks = refs[:pieces]
    out_ref = refs[pieces + added]
    rows = logit_ref.shape[0]
    step = rows // 2
    lane = lax.broadcasted_iota(jnp.int32, (8, LANES), 1)
    weight = jnp.where(lane == 0, 512.0, jnp.where(lane == 1, 2.0, jnp.where(lane == 2, 1.0, 0.0)))
    code = jnp.concatenate([c[:, 2 * columns :] for c in chunks], axis=0)
    ids = lax.dot_general(
        weight.astype(jnp.bfloat16), code, (((1,), (1,)), ((), ())), preferred_element_type=jnp.float32
    )
    ids = ids[:1].astype(jnp.int32) - offset_ref[0]
    copies = []
    for block in range(2):
        span = slice(block * step, (block + 1) * step)
        row = lax.broadcasted_iota(jnp.int32, (step, ids.shape[1]), 0) + block * step
        onehot = jnp.where(row == ids, 1.0, 0.0).astype(jnp.bfloat16)
        left = jnp.concatenate([logit_ref[span, s * LANES : (s + 1) * LANES] for s in spots], axis=1)
        right = jnp.concatenate([c[:, :columns] for c in chunks], axis=0)
        total = jnp.dot(left, right, preferred_element_type=jnp.float32)
        right = jnp.concatenate([c[:, columns : 2 * columns] for c in chunks], axis=0)
        total += jnp.dot(onehot, right, preferred_element_type=jnp.float32)
        if added:
            total += refs[pieces][span, :]
        if last:
            stage, sems = refs[pieces + added + 1 :]
            stage[span, :] = total
            copies.append(pltpu.make_async_copy(stage.at[span, :], out_ref.at[span, :], sems.at[block]))
            copies[-1].start()
        else:
            out_ref[span, :] = total
    for copy in copies:
        copy.wait()


def contract(offset, logits, chunks, spots, columns, partial=None, last=False):
    rows = logits.shape[0]
    added = [] if partial is None else [partial]
    here = pl.BlockSpec(memory_space=pltpu.VMEM)
    scratch = [pltpu.VMEM((rows, columns), jnp.float32), pltpu.SemaphoreType.DMA((2,))]
    return pl.pallas_call(
        functools.partial(contract_kernel, tuple(spots), len(chunks), columns, len(added), last),
        out_shape=jax.ShapeDtypeStruct((rows, columns), jnp.float32),
        in_specs=[pl.BlockSpec(memory_space=pltpu.SMEM)] + [here] * (1 + len(chunks) + len(added)),
        out_specs=pl.BlockSpec(memory_space=pl.ANY) if last else here,
        scratch_shapes=scratch if last else [],
        compiler_params=pltpu.CompilerParams(vmem_limit_bytes=16 << 20),
        cost_estimate=pl.CostEstimate(
            flops=4 * rows * len(spots) * LANES * columns, bytes_accessed=8 << 20, transcendentals=0
        ),
    )(offset, logits, *chunks, *added)


def body(token_ids, hidden, logit_grad, embed_grad):
    dp, vocab = lax.axis_index("dp"), lax.axis_index("vocab")
    columns = hidden.shape[1] // 2
    offset = (vocab * logit_grad.shape[1]).astype(jnp.int32).reshape(1)
    ids = token_ids[:, None]
    lane = lax.broadcasted_iota(jnp.int32, (ROWS, LANES), 1)
    code = jnp.where(lane == 0, ids // 512, jnp.where(lane == 1, (ids // 2) % 256, ids % 2))
    code = jnp.where(lane < 3, code, 0).astype(jnp.bfloat16)

    def payload(side):
        pick = [lax.dynamic_slice_in_dim(a, side * columns, columns, 1) for a in (hidden, embed_grad)]
        return jnp.concatenate(pick + [code], axis=1)

    near, far = arrangement(dp, vocab)
    dims = (((0,), (0,)), ((), ()))
    low, high, early = gather_column(payload(dp), payload(1 - dp))
    held, _ = lax.optimization_barrier((logit_grad, early))
    partner = move(held, fd=1)
    low, high, column = (jnp.concatenate(part, axis=0) for part in (low, high, low + high))
    down_low, up_high = move(low, dx=1), move(high, dx=-1)
    down_high, up_low = move(high, dx=1), move(low, dx=-1)
    across = [move(down_low, dx=1), move(up_high, dx=-1)]
    turned = lax.dot_general(logit_grad, near, dims, preferred_element_type=jnp.float32)
    turned = turned + lax.dot_general(partner, far, dims, preferred_element_type=jnp.float32)
    turned = turned.astype(jnp.bfloat16)
    around = [up_low, up_high, down_low, down_high]
    *around, turned = lax.optimization_barrier((*around, turned))
    first = [column, move(column, fc=1)] + around
    partial = contract(offset, turned, first, (0, 4, 1, 3), columns)
    *across, partial = lax.optimization_barrier((*across, partial))
    second = [move(part, fc=1) for part in around]
    partial = contract(offset, turned, second, (5, 7), columns, partial)
    third = across + [move(part, fc=1) for part in across]
    return contract(offset, turned, third, (2, 6), columns, partial, last=True)


def solution(mesh):
    placed = (
        P(("dp", "vocab")),
        P(("dp", "vocab"), None),
        P("dp", "vocab"),
        P(("dp", "vocab"), None),
    )
    return jax.shard_map(
        body, mesh=mesh, in_specs=placed, out_specs=P("vocab", "dp"), check_vma=False
    )
```

```python
import functools

import jax
import jax.numpy as jnp
import numpy as np
from jax import lax
from jax.experimental import pallas as pl
from jax.experimental.pallas import tpu as pltpu
from jax.sharding import PartitionSpec as P

Z, X, YH, CORE, DP = 8, 4, 2, 2, 2
ROWS = 4
LANES = 128


def coords(vocab):
    return vocab // (X * 4), (vocab // 4) % X, (vocab // 2) % 2, vocab % 2


def flat(dp, z, x, yh, core):
    return dp * (Z * X * 4) + ((z % Z) * X + (x % X)) * 4 + yh * 2 + core


def move(value, dz=0, dx=0, fy=0, fd=0, fc=0):
    pairs = []
    for dp in range(DP):
        for vocab in range(Z * X * 4):
            z, x, yh, core = coords(vocab)
            way = 1 - 2 * core
            pairs.append((flat(dp, z, x, yh, core), flat(dp ^ fd, z + way * dz, x + way * dx, yh ^ fy, core ^ fc)))
    return lax.ppermute(value, ("dp", "vocab"), pairs)


def gather_column(own, other):
    from_dy = move(other, fd=1, fy=1)
    from_dp = move(other, fd=1)
    from_yh = move(own, fy=1)
    chunk = jnp.concatenate([own, from_dp, from_yh, from_dy], axis=0)
    both = jnp.concatenate([chunk, move(chunk, fc=1)], axis=0)
    two, one = move(both, dz=2), move(both, dz=1)
    three, four = move(two, dz=1), move(two[:16], dz=2)
    return jnp.concatenate([chunk, one, two, three, four], axis=0), from_yh


STEPS = (0, 0, 1, 1, 2, -1, -1, 2)
SWAPPED = (0, 1, 0, 1, 0, 1, 0, 1)


def arrangement(dp, vocab):
    z, x, yh, core = coords(vocab)
    place = lax.broadcasted_iota(jnp.int32, (1, 2 * Z * X * YH * CORE * ROWS), 1)
    j, r, part, column = place % 4, (place // 4) % 4, (place // 16) % Z, place // (16 * Z)
    steps, swapped = jnp.zeros_like(place), jnp.zeros_like(place)
    for k in range(len(STEPS)):
        steps = jnp.where(column == k, STEPS[k], steps)
        swapped = jnp.where(column == k, SWAPPED[k], swapped)
    way = 1 - 2 * core
    from_x = (x - way * steps + 2 * X) % X
    holder = core ^ swapped
    back = (part + 1) // 2
    from_z = (z - (1 - 2 * holder) * back + 2 * Z) % Z
    from_core = holder ^ jnp.where((part % 2 == 0) & (part > 0), 1, 0)
    token = ((from_z * X + from_x) * 2 + (yh ^ (r // 2))) * 2 + from_core
    return token * ROWS + j, r % 2


def contract_kernel(spots, pieces, columns, added, last, offset_ref, logit_ref, *refs):
    chunks = refs[:pieces]
    out_ref = refs[pieces + added]
    rows = logit_ref.shape[0]
    step = rows // 2
    lane = lax.broadcasted_iota(jnp.int32, (8, LANES), 1)
    weight = jnp.where(lane == 0, 512.0, jnp.where(lane == 1, 2.0, jnp.where(lane == 2, 1.0, 0.0)))
    code = jnp.concatenate([c[:, 2 * columns :] for c in chunks], axis=0)
    ids = lax.dot_general(
        weight.astype(jnp.bfloat16), code, (((1,), (1,)), ((), ())), preferred_element_type=jnp.float32
    )
    ids = ids[:1].astype(jnp.int32) - offset_ref[0]
    copies = []
    for block in range(2):
        span = slice(block * step, (block + 1) * step)
        row = lax.broadcasted_iota(jnp.int32, (step, ids.shape[1]), 0) + block * step
        onehot = jnp.where(row == ids, 1.0, 0.0).astype(jnp.bfloat16)
        left = jnp.concatenate([logit_ref[span, s * LANES : (s + 1) * LANES] for s in spots], axis=1)
        right = jnp.concatenate([c[:, :columns] for c in chunks], axis=0)
        total = jnp.dot(left, right, preferred_element_type=jnp.float32)
        right = jnp.concatenate([c[:, columns : 2 * columns] for c in chunks], axis=0)
        total += jnp.dot(onehot, right, preferred_element_type=jnp.float32)
        if added:
            total += refs[pieces][span, :]
        if last:
            stage, sems = refs[pieces + added + 1 :]
            stage[span, :] = total
            copies.append(pltpu.make_async_copy(stage.at[span, :], out_ref.at[span, :], sems.at[block]))
            copies[-1].start()
        else:
            out_ref[span, :] = total
    for copy in copies:
        copy.wait()


def contract(offset, logits, chunks, spots, columns, partial=None, last=False):
    rows = logits.shape[0]
    added = [] if partial is None else [partial]
    here = pl.BlockSpec(memory_space=pltpu.VMEM)
    scratch = [pltpu.VMEM((rows, columns), jnp.float32), pltpu.SemaphoreType.DMA((2,))]
    return pl.pallas_call(
        functools.partial(contract_kernel, tuple(spots), len(chunks), columns, len(added), last),
        out_shape=jax.ShapeDtypeStruct((rows, columns), jnp.float32),
        in_specs=[pl.BlockSpec(memory_space=pltpu.SMEM)] + [here] * (1 + len(chunks) + len(added)),
        out_specs=pl.BlockSpec(memory_space=pl.ANY) if last else here,
        scratch_shapes=scratch if last else [],
        compiler_params=pltpu.CompilerParams(vmem_limit_bytes=16 << 20),
        cost_estimate=pl.CostEstimate(
            flops=4 * rows * len(spots) * LANES * columns, bytes_accessed=8 << 20, transcendentals=0
        ),
    )(offset, logits, *chunks, *added)


def body(token_ids, hidden, logit_grad, embed_grad):
    dp, vocab = lax.axis_index("dp"), lax.axis_index("vocab")
    columns = hidden.shape[1] // 2
    offset = (vocab * logit_grad.shape[1]).astype(jnp.int32).reshape(1)
    ids = token_ids[:, None]
    lane = lax.broadcasted_iota(jnp.int32, (ROWS, LANES), 1)
    code = jnp.where(lane == 0, ids // 512, jnp.where(lane == 1, (ids // 2) % 256, ids % 2))
    code = jnp.where(lane < 3, code, 0).astype(jnp.bfloat16)

    def payload(side):
        pick = [lax.dynamic_slice_in_dim(a, side * columns, columns, 1) for a in (hidden, embed_grad)]
        return jnp.concatenate(pick + [code], axis=1)

    dims = (((0,), (0,)), ((), ()))
    token, away = arrangement(dp, vocab)
    own, other, offset, token = lax.optimization_barrier((payload(dp), payload(1 - dp), offset, token))
    spot = lax.broadcasted_iota(jnp.int32, (logit_grad.shape[0], 1), 0)
    near, far = (((spot == token) & (away == side)).astype(jnp.bfloat16) for side in (0, 1))
    column, early = gather_column(own, other)
    held, _ = lax.optimization_barrier((logit_grad, early))
    partner = move(held, fd=1)
    swapped = move(column, fc=1)
    direct = [move(column, dx=1), move(swapped, dx=1)]
    turned = lax.dot_general(logit_grad, near, dims, preferred_element_type=jnp.float32)
    turned = turned + lax.dot_general(partner, far, dims, preferred_element_type=jnp.float32)
    turned = turned.astype(jnp.bfloat16)
    direct[0], turned = lax.optimization_barrier((direct[0], turned))
    passed = move(direct[0], dx=1)
    partial = contract(offset, turned, [column, swapped] + direct, (0, 1, 2, 3), columns)
    passed, partial = lax.optimization_barrier((passed, partial))
    partial = contract(offset, turned, [move(part, fc=1) for part in direct], (5, 6), columns, partial)
    return contract(offset, turned, [passed, move(passed, fc=1)], (4, 7), columns, partial, last=True)


def solution(mesh):
    placed = (
        P(("dp", "vocab")),
        P(("dp", "vocab"), None),
        P("dp", "vocab"),
        P(("dp", "vocab"), None),
    )
    return jax.shard_map(
        body, mesh=mesh, in_specs=placed, out_specs=P("vocab", "dp"), check_vma=False
    )
```

```python
import functools

import jax
import jax.numpy as jnp
import numpy as np
from jax import lax
from jax.experimental import pallas as pl
from jax.experimental.pallas import tpu as pltpu
from jax.sharding import PartitionSpec as P

Z, X, YH, CORE, DP = 8, 4, 2, 2, 2
ROWS = 4
LANES = 128
TOKENS = 128
SLOTS = 32
CODES = 16


def coords(vocab):
    return vocab // (X * 4), (vocab // 4) % X, (vocab // 2) % 2, vocab % 2


def flat(dp, z, x, yh, core):
    return dp * (Z * X * 4) + ((z % Z) * X + (x % X)) * 4 + yh * 2 + core


def move(value, dz=0, dx=0, fy=0, fd=0, fc=0):
    pairs = []
    for dp in range(DP):
        for vocab in range(Z * X * 4):
            z, x, yh, core = coords(vocab)
            way = 1 - 2 * core
            pairs.append((flat(dp, z, x, yh, core), flat(dp ^ fd, z + way * dz, x + way * dx, yh ^ fy, core ^ fc)))
    return lax.ppermute(value, ("dp", "vocab"), pairs)


def gather_column(own, other):
    from_dy = move(other, fd=1, fy=1)
    from_dp = move(other, fd=1)
    from_yh = move(own, fy=1)
    chunk = jnp.concatenate([own, from_dp, from_yh, from_dy], axis=0)
    both = jnp.concatenate([chunk, move(chunk, fc=1)], axis=0)
    two, one = move(both, dz=2), move(both, dz=1)
    three, four = move(two, dz=1), move(two[:16], dz=2)
    return [chunk, one, two, three, four], from_yh


STEPS = (0, 0, 1, 1, 2, -1, -1, 2)
SWAPPED = (0, 1, 0, 1, 0, 1, 0, 1)


def arrangement(dp, vocab):
    z, x, yh, core = coords(vocab)
    place = lax.broadcasted_iota(jnp.int32, (1, 2 * Z * X * YH * CORE * ROWS), 1)
    j, r, part, column = place % 4, (place // 4) % 4, (place // 16) % Z, place // (16 * Z)
    steps, swapped = jnp.zeros_like(place), jnp.zeros_like(place)
    for k in range(len(STEPS)):
        steps = jnp.where(column == k, STEPS[k], steps)
        swapped = jnp.where(column == k, SWAPPED[k], swapped)
    way = 1 - 2 * core
    from_x = (x - way * steps + 2 * X) % X
    holder = core ^ swapped
    back = (part + 1) // 2
    from_z = (z - (1 - 2 * holder) * back + 2 * Z) % Z
    from_core = holder ^ jnp.where((part % 2 == 0) & (part > 0), 1, 0)
    token = ((from_z * X + from_x) * 2 + (yh ^ (r // 2))) * 2 + from_core
    return token * ROWS + j, r % 2


def pack_kernel(columns, plane_ref, *refs):
    parts, (out_ref, rest_ref) = refs[:-2], refs[-2:]
    side = (((1,), (1,)), ((), ()))
    out_ref[:TOKENS, :] = jnp.concatenate([p[:, :columns] for p in parts], axis=0)
    grads = jnp.concatenate([p[:, columns : 2 * columns] for p in parts], axis=0)
    codes = jnp.concatenate([p[:, 2 * columns :] for p in parts], axis=0)
    line = lax.broadcasted_iota(jnp.int32, (CODES, LANES), 0)
    lane = lax.broadcasted_iota(jnp.int32, (CODES, LANES), 1)
    pick = jnp.where(line == lane, 1.0, 0.0).astype(jnp.bfloat16)
    turned = lax.dot_general(pick, codes, side, preferred_element_type=jnp.float32)
    top = turned[:1].astype(jnp.int32)
    match = ((top >> 5) == plane_ref[0]) & (((top >> 2) & 1) == plane_ref[1])
    found = jnp.where(match, 1.0, 0.0)
    row = lax.broadcasted_iota(jnp.int32, (TOKENS, TOKENS), 0)
    col = lax.broadcasted_iota(jnp.int32, (TOKENS, TOKENS), 1)
    before = jnp.where(row < col, 1.0, 0.0).astype(jnp.bfloat16)
    many = jnp.broadcast_to(found, (CODES, TOKENS)).astype(jnp.bfloat16)
    rank = jnp.dot(many, before, preferred_element_type=jnp.float32)[:1].astype(jnp.int32)
    rank = jnp.where(match, rank, -1)
    over = jnp.max(jnp.where(rank >= SLOTS, 1.0, 0.0), axis=1, keepdims=True)
    turned = jnp.where(line == 3, 1.0, turned).astype(jnp.bfloat16)
    for ref, start, first, slots in ((out_ref, TOKENS, 0, SLOTS), (rest_ref, 0, SLOTS, TOKENS - SLOTS)):
        chosen = jnp.where(rank == row[:slots] + first, 1.0, 0.0).astype(jnp.bfloat16)
        ref[start : start + slots, :] = jnp.dot(chosen, grads, preferred_element_type=jnp.float32).astype(jnp.bfloat16)
        chosen = jnp.where(rank == row + first, 1.0, 0.0).astype(jnp.bfloat16)
        code = lax.dot_general(turned, chosen, side, preferred_element_type=jnp.float32)
        code = jnp.where(line == 4, over, code).astype(jnp.bfloat16)
        ref[start + slots : start + slots + CODES, :LANES] = code
        ref[start + slots : start + slots + CODES, LANES:] = jnp.zeros((CODES, columns - LANES), jnp.bfloat16)


def pack(plane, parts, columns):
    here = pl.BlockSpec(memory_space=pltpu.VMEM)
    shapes = (TOKENS + SLOTS + CODES, TOKENS - SLOTS + CODES)
    return pl.pallas_call(
        functools.partial(pack_kernel, columns),
        out_shape=[jax.ShapeDtypeStruct((rows, columns), jnp.bfloat16) for rows in shapes],
        in_specs=[pl.BlockSpec(memory_space=pltpu.SMEM)] + [here] * len(parts),
        out_specs=[here, here],
        compiler_params=pltpu.CompilerParams(vmem_limit_bytes=8 << 20),
        cost_estimate=pl.CostEstimate(flops=1 << 26, bytes_accessed=2 << 20, transcendentals=0),
    )(plane, *parts)


def slot_ids(chunks, first, slots, offset):
    ids = []
    for c in chunks:
        code = c[first + slots : first + slots + CODES, :LANES].astype(jnp.float32)
        row = (code[:1] * 512.0 + code[1:2] * 2.0 + code[2:3]).astype(jnp.int32) - offset
        ids.append(jnp.where(code[3:4] > 0.5, row, -1)[:, :slots])
    return jnp.concatenate(ids, axis=1)


def contract_kernel(spots, added, others, offset_ref, logit_ref, *refs):
    pieces = len(spots)
    chunks = refs[:pieces]
    out_ref = refs[pieces + added + others]
    rows = logit_ref.shape[0]
    step = rows // 2
    ids = slot_ids(chunks, TOKENS, SLOTS, offset_ref[0])
    copies = []
    for block in range(2):
        span = slice(block * step, (block + 1) * step)
        row = lax.broadcasted_iota(jnp.int32, (step, ids.shape[1]), 0) + block * step
        onehot = jnp.where(row == ids, 1.0, 0.0).astype(jnp.bfloat16)
        left = jnp.concatenate([logit_ref[span, s * LANES : (s + 1) * LANES] for s in spots], axis=1)
        right = jnp.concatenate([c[:TOKENS, :] for c in chunks], axis=0)
        total = jnp.dot(left, right, preferred_element_type=jnp.float32)
        right = jnp.concatenate([c[TOKENS : TOKENS + SLOTS, :] for c in chunks], axis=0)
        total += jnp.dot(onehot, right, preferred_element_type=jnp.float32)
        if added:
            total += refs[pieces][span, :]
        if others:
            over_ref, stage, sems = refs[pieces + added + others + 1 :]
            stage[span, :] = total
            copies.append(pltpu.make_async_copy(stage.at[span, :], out_ref.at[span, :], sems.at[block]))
            copies[-1].start()
        else:
            out_ref[span, :] = total
    if others:
        over = [c[TOKENS + SLOTS : TOKENS + SLOTS + CODES, :LANES] for c in chunks + refs[pieces + added :][:others]]
        over = functools.reduce(jnp.maximum, [c.astype(jnp.float32)[4:5] for c in over])
        over_ref[...] = jnp.broadcast_to(over, over_ref.shape).astype(jnp.int32)
    for copy in copies:
        copy.wait()


def contract(offset, logits, chunks, spots, partial=None, others=()):
    rows, columns = logits.shape[0], chunks[0].shape[1]
    added = [] if partial is None else [partial]
    here = pl.BlockSpec(memory_space=pltpu.VMEM)
    out = jax.ShapeDtypeStruct((rows, columns), jnp.float32)
    scratch = [pltpu.VMEM((rows, columns), jnp.float32), pltpu.SemaphoreType.DMA((2,))]
    return pl.pallas_call(
        functools.partial(contract_kernel, tuple(spots), len(added), len(others)),
        out_shape=[out, jax.ShapeDtypeStruct((8, LANES), jnp.int32)] if others else out,
        in_specs=[pl.BlockSpec(memory_space=pltpu.SMEM)] + [here] * (1 + len(chunks) + len(added) + len(others)),
        out_specs=[pl.BlockSpec(memory_space=pl.ANY), here] if others else here,
        scratch_shapes=scratch if others else [],
        compiler_params=pltpu.CompilerParams(vmem_limit_bytes=16 << 20),
        cost_estimate=pl.CostEstimate(
            flops=3 * rows * len(spots) * LANES * columns, bytes_accessed=8 << 20, transcendentals=0
        ),
    )(offset, logits, *chunks, *added, *others)


def append_kernel(pieces, slots, offset_ref, *refs):
    chunks, base_ref, out_ref = refs[:pieces], refs[pieces], refs[pieces + 1]
    rows = out_ref.shape[0]
    ids = slot_ids(chunks, 0, slots, offset_ref[0] + pl.program_id(0) * rows)
    row = lax.broadcasted_iota(jnp.int32, (rows, ids.shape[1]), 0)
    onehot = jnp.where(row == ids, 1.0, 0.0).astype(jnp.bfloat16)
    right = jnp.concatenate([c[:slots, :] for c in chunks], axis=0)
    out_ref[...] = base_ref[...] + jnp.dot(onehot, right, preferred_element_type=jnp.float32)


def append(offset, chunks, base):
    rows, columns = base.shape
    block = rows // 4
    whole = pl.BlockSpec(chunks[0].shape, lambda m: (0, 0), pipeline_mode=pl.Buffered(1))
    tile = pl.BlockSpec((block, columns), lambda m: (m, 0))
    return pl.pallas_call(
        functools.partial(append_kernel, len(chunks), chunks[0].shape[0] - CODES),
        out_shape=jax.ShapeDtypeStruct(base.shape, base.dtype),
        grid=(rows // block,),
        in_specs=[pl.BlockSpec(memory_space=pltpu.SMEM)] + [whole] * len(chunks) + [tile],
        out_specs=tile,
        input_output_aliases={1 + len(chunks): 0},
        compiler_params=pltpu.CompilerParams(vmem_limit_bytes=16 << 20),
    )(offset, *chunks, base)


def body(token_ids, hidden, logit_grad, embed_grad):
    dp, vocab = lax.axis_index("dp"), lax.axis_index("vocab")
    columns = hidden.shape[1] // 2
    offset = (vocab * logit_grad.shape[1]).astype(jnp.int32).reshape(1)
    ids = token_ids[:, None]
    lane = lax.broadcasted_iota(jnp.int32, (ROWS, LANES), 1)
    code = jnp.where(lane == 0, ids // 512, jnp.where(lane == 1, (ids // 2) % 256, ids % 2))
    code = jnp.where(lane < 3, code, 0).astype(jnp.bfloat16)

    def payload(side):
        pick = [lax.dynamic_slice_in_dim(a, side * columns, columns, 1) for a in (hidden, embed_grad)]
        return jnp.concatenate(pick + [code], axis=1)

    dims = (((0,), (0,)), ((), ()))
    token, away = arrangement(dp, vocab)
    z, _, yh, _ = coords(vocab)
    plane = jnp.stack([z, yh]).astype(jnp.int32)
    own, other, offset, token, plane = lax.optimization_barrier(
        (payload(dp), payload(1 - dp), offset, token, plane)
    )
    spot = lax.broadcasted_iota(jnp.int32, (logit_grad.shape[0], 1), 0)
    near, far = (((spot == token) & (away == side)).astype(jnp.bfloat16) for side in (0, 1))
    parts, early = gather_column(own, other)
    held, _ = lax.optimization_barrier((logit_grad, early))
    partner = move(held, fd=1)
    column, rest = pack(plane, parts, columns)
    swapped = move(column, fc=1)
    direct = [move(column, dx=1), move(swapped, dx=1)]
    local, _ = lax.optimization_barrier((logit_grad, swapped))
    turned = lax.dot_general(local, near, dims, preferred_element_type=jnp.float32)
    turned = turned + lax.dot_general(partner, far, dims, preferred_element_type=jnp.float32)
    turned = turned.astype(jnp.bfloat16)
    direct[0], turned = lax.optimization_barrier((direct[0], turned))
    passed = move(direct[0], dx=1)
    first = [column, swapped] + direct
    partial = contract(offset, turned, first, (0, 1, 2, 3))
    passed, partial = lax.optimization_barrier((passed, partial))
    second = [move(part, fc=1) for part in direct]
    partial = contract(offset, turned, second, (5, 6), partial)
    result, over = contract(offset, turned, [passed, move(passed, fc=1)], (4, 7), partial, first + second)

    def again(state):
        total, _ = state
        pair = [rest, move(rest, fc=1)]
        came = [move(part, dx=1) for part in pair]
        came.append(move(came[0], dx=1))
        return append(offset, pair + came + [move(part, fc=1) for part in came], total), jnp.int32(0)

    return lax.while_loop(lambda state: state[1] > 0, again, (result, over[0, 0]))[0]


def solution(mesh):
    placed = (
        P(("dp", "vocab")),
        P(("dp", "vocab"), None),
        P("dp", "vocab"),
        P(("dp", "vocab"), None),
    )
    return jax.shard_map(
        body, mesh=mesh, in_specs=placed, out_specs=P("vocab", "dp"), check_vma=False
    )
```

```python
import functools

import jax
import jax.numpy as jnp
import numpy as np
from jax import lax
from jax.experimental import pallas as pl
from jax.experimental.pallas import tpu as pltpu
from jax.sharding import PartitionSpec as P

Z, X, YH, CORE, DP = 8, 4, 2, 2, 2
ROWS = 4
LANES = 128
TOKENS = 128
SLOTS = 32
CODES = 16


def coords(vocab):
    return vocab // (X * 4), (vocab // 4) % X, (vocab // 2) % 2, vocab % 2


def flat(dp, z, x, yh, core):
    return dp * (Z * X * 4) + ((z % Z) * X + (x % X)) * 4 + yh * 2 + core


def move(value, dz=0, dx=0, fy=0, fd=0, fc=0):
    pairs = []
    for dp in range(DP):
        for vocab in range(Z * X * 4):
            z, x, yh, core = coords(vocab)
            way = 1 - 2 * core
            pairs.append((flat(dp, z, x, yh, core), flat(dp ^ fd, z + way * dz, x + way * dx, yh ^ fy, core ^ fc)))
    return lax.ppermute(value, ("dp", "vocab"), pairs)


def gather_column(own, other):
    from_dy = move(other, fd=1, fy=1)
    from_dp = move(other, fd=1)
    from_yh = move(own, fy=1)
    chunk = jnp.concatenate([own, from_dp, from_yh, from_dy], axis=0)
    both = jnp.concatenate([chunk, move(chunk, fc=1)], axis=0)
    two, one = move(both, dz=2), move(both, dz=1)
    three, four = move(two, dz=1), move(two[:16], dz=2)
    return [chunk, one, two, three, four], from_yh


STEPS = (0, 0, 1, 1, 2, -1, -1, 2)
SWAPPED = (0, 1, 0, 1, 0, 1, 0, 1)


def arrangement(dp, vocab):
    z, x, yh, core = coords(vocab)
    place = lax.broadcasted_iota(jnp.int32, (1, 2 * Z * X * YH * CORE * ROWS), 1)
    j, r, part, column = place % 4, (place // 4) % 4, (place // 16) % Z, place // (16 * Z)
    steps, swapped = jnp.zeros_like(place), jnp.zeros_like(place)
    for k in range(len(STEPS)):
        steps = jnp.where(column == k, STEPS[k], steps)
        swapped = jnp.where(column == k, SWAPPED[k], swapped)
    way = 1 - 2 * core
    from_x = (x - way * steps + 2 * X) % X
    holder = core ^ swapped
    back = (part + 1) // 2
    from_z = (z - (1 - 2 * holder) * back + 2 * Z) % Z
    from_core = holder ^ jnp.where((part % 2 == 0) & (part > 0), 1, 0)
    token = ((from_z * X + from_x) * 2 + (yh ^ (r // 2))) * 2 + from_core
    return token * ROWS + j, r % 2


def payload_kernel(dp_ref, *refs):
    own_ref, other_ref, ids_ref, hidden_ref, grad_ref, sems = refs[3:]
    copies = [pltpu.make_async_copy(a, b, sems.at[k]) for k, (a, b) in enumerate(zip(refs[:3], refs[5:8]))]
    for copy in copies:
        copy.start()
    for copy in copies:
        copy.wait()
    columns = hidden_ref.shape[1] // 2
    row = lax.broadcasted_iota(jnp.int32, (ROWS, LANES), 0)
    lane = lax.broadcasted_iota(jnp.int32, (ROWS, LANES), 1)
    ids = jnp.zeros((ROWS, LANES), jnp.int32)
    for k in range(ROWS):
        ids = jnp.where(row == k, ids_ref[k], ids)
    code = jnp.where(lane == 0, ids >> 9, jnp.where(lane == 1, (ids >> 1) & 255, ids & 1))
    code = jnp.where(lane < 3, code, 0).astype(jnp.float32).astype(jnp.bfloat16)
    for side, refs in ((0, (own_ref, other_ref)), (1, (other_ref, own_ref))):

        @pl.when(dp_ref[0] == side)
        def _():
            for half, ref in enumerate(refs):
                span = slice(half * columns, (half + 1) * columns)
                ref[:, :columns] = hidden_ref[:, span]
                ref[:, columns : 2 * columns] = grad_ref[:, span]

    own_ref[:, 2 * columns :] = code
    other_ref[:, 2 * columns :] = code


def payloads(dp, ids, hidden, grads):
    here, scalars = pl.BlockSpec(memory_space=pltpu.VMEM), pl.BlockSpec(memory_space=pltpu.SMEM)
    shape = jax.ShapeDtypeStruct((ROWS, hidden.shape[1] + LANES), jnp.bfloat16)
    held = [pltpu.SMEM(ids.shape, ids.dtype), pltpu.VMEM(hidden.shape, hidden.dtype), pltpu.VMEM(grads.shape, grads.dtype)]
    return pl.pallas_call(
        payload_kernel,
        out_shape=[shape, shape],
        in_specs=[scalars] + [pl.BlockSpec(memory_space=pltpu.HBM)] * 3,
        out_specs=[here, here],
        scratch_shapes=held + [pltpu.SemaphoreType.DMA((3,))],
        compiler_params=pltpu.CompilerParams(vmem_limit_bytes=4 << 20),
    )(dp, ids, hidden, grads)


def pack_kernel(columns, plane_ref, *refs):
    parts, (out_ref, rest_ref) = refs[:-2], refs[-2:]
    side = (((1,), (1,)), ((), ()))
    out_ref[:TOKENS, :] = jnp.concatenate([p[:, :columns] for p in parts], axis=0)
    grads = jnp.concatenate([p[:, columns : 2 * columns] for p in parts], axis=0)
    codes = jnp.concatenate([p[:, 2 * columns :] for p in parts], axis=0)
    line = lax.broadcasted_iota(jnp.int32, (CODES, LANES), 0)
    lane = lax.broadcasted_iota(jnp.int32, (CODES, LANES), 1)
    pick = jnp.where(line == lane, 1.0, 0.0).astype(jnp.bfloat16)
    turned = lax.dot_general(pick, codes, side, preferred_element_type=jnp.float32)
    top = turned[:1].astype(jnp.int32)
    match = ((top >> 5) == plane_ref[0]) & (((top >> 2) & 1) == plane_ref[1])
    found = jnp.where(match, 1.0, 0.0)
    row = lax.broadcasted_iota(jnp.int32, (TOKENS, TOKENS), 0)
    col = lax.broadcasted_iota(jnp.int32, (TOKENS, TOKENS), 1)
    before = jnp.where(row < col, 1.0, 0.0).astype(jnp.bfloat16)
    many = jnp.broadcast_to(found, (CODES, TOKENS)).astype(jnp.bfloat16)
    rank = jnp.dot(many, before, preferred_element_type=jnp.float32)[:1].astype(jnp.int32)
    rank = jnp.where(match, rank, -1)
    over = jnp.max(jnp.where(rank >= SLOTS, 1.0, 0.0), axis=1, keepdims=True)
    turned = jnp.where(line == 3, 1.0, turned).astype(jnp.bfloat16)
    for ref, start, first, slots in ((out_ref, TOKENS, 0, SLOTS), (rest_ref, 0, SLOTS, TOKENS - SLOTS)):
        chosen = jnp.where(rank == row[:slots] + first, 1.0, 0.0).astype(jnp.bfloat16)
        ref[start : start + slots, :] = jnp.dot(chosen, grads, preferred_element_type=jnp.float32).astype(jnp.bfloat16)
        chosen = jnp.where(rank == row + first, 1.0, 0.0).astype(jnp.bfloat16)
        code = lax.dot_general(turned, chosen, side, preferred_element_type=jnp.float32)
        code = jnp.where(line == 4, over, code).astype(jnp.bfloat16)
        ref[start + slots : start + slots + CODES, :LANES] = code
        ref[start + slots : start + slots + CODES, LANES:] = jnp.zeros((CODES, columns - LANES), jnp.bfloat16)


def pack(plane, parts, columns):
    here = pl.BlockSpec(memory_space=pltpu.VMEM)
    shapes = (TOKENS + SLOTS + CODES, TOKENS - SLOTS + CODES)
    return pl.pallas_call(
        functools.partial(pack_kernel, columns),
        out_shape=[jax.ShapeDtypeStruct((rows, columns), jnp.bfloat16) for rows in shapes],
        in_specs=[pl.BlockSpec(memory_space=pltpu.SMEM)] + [here] * len(parts),
        out_specs=[here, here],
        compiler_params=pltpu.CompilerParams(vmem_limit_bytes=8 << 20),
        cost_estimate=pl.CostEstimate(flops=1 << 26, bytes_accessed=2 << 20, transcendentals=0),
    )(plane, *parts)


def slot_ids(chunks, first, slots, offset):
    ids = []
    for c in chunks:
        code = c[first + slots : first + slots + CODES, :LANES].astype(jnp.float32)
        row = (code[:1] * 512.0 + code[1:2] * 2.0 + code[2:3]).astype(jnp.int32) - offset
        ids.append(jnp.where(code[3:4] > 0.5, row, -1)[:, :slots])
    return jnp.concatenate(ids, axis=1)


def contract_kernel(spots, added, others, offset_ref, logit_ref, *refs):
    pieces = len(spots)
    chunks = refs[:pieces]
    out_ref = refs[pieces + added + others]
    rows = logit_ref.shape[0]
    step = rows // 2
    ids = slot_ids(chunks, TOKENS, SLOTS, offset_ref[0])
    copies = []
    for block in range(2):
        span = slice(block * step, (block + 1) * step)
        row = lax.broadcasted_iota(jnp.int32, (step, ids.shape[1]), 0) + block * step
        onehot = jnp.where(row == ids, 1.0, 0.0).astype(jnp.bfloat16)
        left = [logit_ref[span, s * LANES : (s + 1) * LANES] for s in spots]
        right = jnp.concatenate([c[:TOKENS, :] for c in chunks] + [c[TOKENS : TOKENS + SLOTS, :] for c in chunks], axis=0)
        total = jnp.dot(jnp.concatenate(left + [onehot], axis=1), right, preferred_element_type=jnp.float32)
        if added:
            total += refs[pieces][span, :]
        if others:
            over_ref, stage, sems = refs[pieces + added + others + 1 :]
            stage[span, :] = total
            copies.append(pltpu.make_async_copy(stage.at[span, :], out_ref.at[span, :], sems.at[block]))
            copies[-1].start()
        else:
            out_ref[span, :] = total
    if others:
        over = [c[TOKENS + SLOTS : TOKENS + SLOTS + CODES, :LANES] for c in chunks + refs[pieces + added :][:others]]
        over = functools.reduce(jnp.maximum, [c.astype(jnp.float32)[4:5] for c in over])
        over_ref[0] = jnp.max(over).astype(jnp.int32)
    for copy in copies:
        copy.wait()


def contract(offset, logits, chunks, spots, partial=None, others=()):
    rows, columns = logits.shape[0], chunks[0].shape[1]
    added = [] if partial is None else [partial]
    here = pl.BlockSpec(memory_space=pltpu.VMEM)
    out = jax.ShapeDtypeStruct((rows, columns), jnp.float32)
    scratch = [pltpu.VMEM((rows, columns), jnp.float32), pltpu.SemaphoreType.DMA((2,))]
    return pl.pallas_call(
        functools.partial(contract_kernel, tuple(spots), len(added), len(others)),
        out_shape=[out, jax.ShapeDtypeStruct((1,), jnp.int32)] if others else out,
        in_specs=[pl.BlockSpec(memory_space=pltpu.SMEM)] + [here] * (1 + len(chunks) + len(added) + len(others)),
        out_specs=[pl.BlockSpec(memory_space=pl.ANY), pl.BlockSpec(memory_space=pltpu.SMEM)] if others else here,
        scratch_shapes=scratch if others else [],
        compiler_params=pltpu.CompilerParams(vmem_limit_bytes=16 << 20),
        cost_estimate=pl.CostEstimate(
            flops=3 * rows * len(spots) * LANES * columns, bytes_accessed=8 << 20, transcendentals=0
        ),
    )(offset, logits, *chunks, *added, *others)


def append_kernel(pieces, slots, offset_ref, *refs):
    chunks, base_ref, out_ref = refs[:pieces], refs[pieces], refs[pieces + 1]
    rows = out_ref.shape[0]
    ids = slot_ids(chunks, 0, slots, offset_ref[0] + pl.program_id(0) * rows)
    row = lax.broadcasted_iota(jnp.int32, (rows, ids.shape[1]), 0)
    onehot = jnp.where(row == ids, 1.0, 0.0).astype(jnp.bfloat16)
    right = jnp.concatenate([c[:slots, :] for c in chunks], axis=0)
    out_ref[...] = base_ref[...] + jnp.dot(onehot, right, preferred_element_type=jnp.float32)


def append(offset, chunks, base):
    rows, columns = base.shape
    block = rows // 4
    whole = pl.BlockSpec(chunks[0].shape, lambda m: (0, 0), pipeline_mode=pl.Buffered(1))
    tile = pl.BlockSpec((block, columns), lambda m: (m, 0))
    return pl.pallas_call(
        functools.partial(append_kernel, len(chunks), chunks[0].shape[0] - CODES),
        out_shape=jax.ShapeDtypeStruct(base.shape, base.dtype),
        grid=(rows // block,),
        in_specs=[pl.BlockSpec(memory_space=pltpu.SMEM)] + [whole] * len(chunks) + [tile],
        out_specs=tile,
        input_output_aliases={1 + len(chunks): 0},
        compiler_params=pltpu.CompilerParams(vmem_limit_bytes=16 << 20),
    )(offset, *chunks, base)


def body(token_ids, hidden, logit_grad, embed_grad):
    dp, vocab = lax.axis_index("dp"), lax.axis_index("vocab")
    columns = hidden.shape[1] // 2
    offset = (vocab * logit_grad.shape[1]).astype(jnp.int32).reshape(1)
    dims = (((0,), (0,)), ((), ()))
    token, away = arrangement(dp, vocab)
    z, _, yh, _ = coords(vocab)
    plane = jnp.stack([z, yh]).astype(jnp.int32)
    own, other = payloads(dp.astype(jnp.int32).reshape(1), token_ids, hidden, embed_grad)
    own, other, offset, token, plane = lax.optimization_barrier((own, other, offset, token, plane))
    spot = lax.broadcasted_iota(jnp.int32, (logit_grad.shape[0], 1), 0)
    near, far = (((spot == token) & (away == side)).astype(jnp.bfloat16) for side in (0, 1))
    parts, early = gather_column(own, other)
    held, _ = lax.optimization_barrier((logit_grad, early))
    partner = move(held, fd=1)
    column, rest = pack(plane, parts, columns)
    swapped = move(column, fc=1)
    direct = move(column, dx=1)
    local, _ = lax.optimization_barrier((logit_grad, swapped))
    turned = lax.dot_general(local, near, dims, preferred_element_type=jnp.float32)
    turned = turned + lax.dot_general(partner, far, dims, preferred_element_type=jnp.float32)
    late, turned = lax.optimization_barrier((swapped, turned.astype(jnp.bfloat16)))
    passed = move(direct, dx=1)
    direct = [direct, move(late, dx=1)]
    first = [column, swapped] + direct
    partial = contract(offset, turned, first, (0, 1, 2, 3))
    passed, partial = lax.optimization_barrier((passed, partial))
    second = [passed] + [move(part, fc=1) for part in direct]
    partial = contract(offset, turned, second, (4, 5, 6), partial)
    result, over = contract(offset, turned, [move(passed, fc=1)], (7,), partial, first + second)

    def again(state):
        total, _ = state
        pair = [rest, move(rest, fc=1)]
        came = [move(part, dx=1) for part in pair]
        came.append(move(came[0], dx=1))
        return append(offset, pair + came + [move(part, fc=1) for part in came], total), jnp.int32(0)

    return lax.while_loop(lambda state: state[1] > 0, again, (result, over[0]))[0]


def solution(mesh):
    placed = (
        P(("dp", "vocab")),
        P(("dp", "vocab"), None),
        P("dp", "vocab"),
        P(("dp", "vocab"), None),
    )
    return jax.shard_map(
        body, mesh=mesh, in_specs=placed, out_specs=P("vocab", "dp"), check_vma=False
    )
```

```python
import functools

import jax
import jax.numpy as jnp
import numpy as np
from jax import lax
from jax.experimental import pallas as pl
from jax.experimental.pallas import tpu as pltpu
from jax.sharding import PartitionSpec as P

Z, X, YH, CORE, DP = 8, 4, 2, 2, 2
ROWS = 4
LANES = 128
TOKENS = 128
SLOTS = 32
CODES = 8


def coords(vocab):
    return vocab // (X * 4), (vocab // 4) % X, (vocab // 2) % 2, vocab % 2


def flat(dp, z, x, yh, core):
    return dp * (Z * X * 4) + ((z % Z) * X + (x % X)) * 4 + yh * 2 + core


def move(value, dz=0, dx=0, fy=0, fd=0, fc=0):
    pairs = []
    for dp in range(DP):
        for vocab in range(Z * X * 4):
            z, x, yh, core = coords(vocab)
            way = 1 - 2 * core
            pairs.append((flat(dp, z, x, yh, core), flat(dp ^ fd, z + way * dz, x + way * dx, yh ^ fy, core ^ fc)))
    return lax.ppermute(value, ("dp", "vocab"), pairs)


def gather_column(own, other):
    from_dy = move(other, fd=1, fy=1)
    from_dp = move(other, fd=1)
    from_yh = move(own, fy=1)
    chunk = jnp.concatenate([own, from_dp, from_yh, from_dy], axis=0)
    both = jnp.concatenate([chunk, move(chunk, fc=1)], axis=0)
    two, one = move(both, dz=2), move(both, dz=1)
    three, four = move(two, dz=1), move(two[:16], dz=2)
    return [chunk, one, two, three, four], from_yh


STEPS = (0, 0, 1, 1, 2, -1, -1, 2)
SWAPPED = (0, 1, 0, 1, 0, 1, 0, 1)


def arrangement(dp, vocab):
    z, x, yh, core = coords(vocab)
    place = lax.broadcasted_iota(jnp.int32, (1, 2 * Z * X * YH * CORE * ROWS), 1)
    j, r, part, column = place % 4, (place // 4) % 4, (place // 16) % Z, place // (16 * Z)
    steps, swapped = jnp.zeros_like(place), jnp.zeros_like(place)
    for k in range(len(STEPS)):
        steps = jnp.where(column == k, STEPS[k], steps)
        swapped = jnp.where(column == k, SWAPPED[k], swapped)
    way = 1 - 2 * core
    from_x = (x - way * steps + 2 * X) % X
    holder = core ^ swapped
    back = (part + 1) // 2
    from_z = (z - (1 - 2 * holder) * back + 2 * Z) % Z
    from_core = holder ^ jnp.where((part % 2 == 0) & (part > 0), 1, 0)
    token = ((from_z * X + from_x) * 2 + (yh ^ (r // 2))) * 2 + from_core
    return token * ROWS + j, r % 2


def pack_kernel(columns, plane_ref, *refs):
    parts, (out_ref, rest_ref) = refs[:-2], refs[-2:]
    side = (((1,), (1,)), ((), ()))
    out_ref[:TOKENS, :] = jnp.concatenate([p[:, :columns] for p in parts], axis=0)
    grads = jnp.concatenate([p[:, columns : 2 * columns] for p in parts], axis=0)
    codes = jnp.concatenate([p[:, 2 * columns :] for p in parts], axis=0)
    line = lax.broadcasted_iota(jnp.int32, (CODES, LANES), 0)
    lane = lax.broadcasted_iota(jnp.int32, (CODES, LANES), 1)
    pick = jnp.where(line == lane, 1.0, 0.0).astype(jnp.bfloat16)
    turned = lax.dot_general(pick, codes, side, preferred_element_type=jnp.float32)
    top = turned[:1].astype(jnp.int32)
    match = ((top >> 5) == plane_ref[0]) & (((top >> 2) & 1) == plane_ref[1])
    found = jnp.where(match, 1.0, 0.0)
    row = lax.broadcasted_iota(jnp.int32, (TOKENS, TOKENS), 0)
    col = lax.broadcasted_iota(jnp.int32, (TOKENS, TOKENS), 1)
    before = jnp.where(row < col, 1.0, 0.0).astype(jnp.bfloat16)
    many = jnp.broadcast_to(found, (CODES, TOKENS)).astype(jnp.bfloat16)
    rank = jnp.dot(many, before, preferred_element_type=jnp.float32)[:1].astype(jnp.int32)
    rank = jnp.where(match, rank, -1)
    over = jnp.max(jnp.where(rank >= SLOTS, 1.0, 0.0), axis=1, keepdims=True)
    turned = jnp.where(line == 3, 1.0, turned).astype(jnp.bfloat16)
    for ref, start, first, slots in ((out_ref, TOKENS, 0, SLOTS), (rest_ref, 0, SLOTS, TOKENS - SLOTS)):
        chosen = jnp.where(rank == row[:slots] + first, 1.0, 0.0).astype(jnp.bfloat16)
        ref[start : start + slots, :] = jnp.dot(chosen, grads, preferred_element_type=jnp.float32).astype(jnp.bfloat16)
        chosen = jnp.where(rank == row + first, 1.0, 0.0).astype(jnp.bfloat16)
        code = lax.dot_general(turned, chosen, side, preferred_element_type=jnp.float32)
        code = jnp.where(line == 4, over, code).astype(jnp.bfloat16)
        ref[start + slots : start + slots + CODES, :LANES] = code
        ref[start + slots : start + slots + CODES, LANES:] = jnp.zeros((CODES, columns - LANES), jnp.bfloat16)


def pack(plane, parts, columns):
    here = pl.BlockSpec(memory_space=pltpu.VMEM)
    shapes = (TOKENS + SLOTS + CODES, TOKENS - SLOTS + CODES)
    return pl.pallas_call(
        functools.partial(pack_kernel, columns),
        out_shape=[jax.ShapeDtypeStruct((rows, columns), jnp.bfloat16) for rows in shapes],
        in_specs=[pl.BlockSpec(memory_space=pltpu.SMEM)] + [here] * len(parts),
        out_specs=[here, here],
        compiler_params=pltpu.CompilerParams(vmem_limit_bytes=8 << 20),
        cost_estimate=pl.CostEstimate(flops=1 << 26, bytes_accessed=2 << 20, transcendentals=0),
    )(plane, *parts)


def slot_ids(chunks, first, slots, offset):
    ids = []
    for c in chunks:
        code = c[first + slots : first + slots + CODES, :LANES].astype(jnp.float32)
        row = (code[:1] * 512.0 + code[1:2] * 2.0 + code[2:3]).astype(jnp.int32) - offset
        ids.append(jnp.where(code[3:4] > 0.5, row, -1)[:, :slots])
    return jnp.concatenate(ids, axis=1)


def contract_kernel(spots, added, others, offset_ref, logit_ref, *refs):
    pieces = len(spots)
    chunks = refs[:pieces]
    out_ref = refs[pieces + added + others]
    rows = logit_ref.shape[0]
    blocks = 8 if others else 2
    step = rows // blocks
    ids = slot_ids(chunks, TOKENS, SLOTS, offset_ref[0])
    copies = []
    for block in range(blocks):
        span = slice(block * step, (block + 1) * step)
        row = lax.broadcasted_iota(jnp.int32, (step, ids.shape[1]), 0) + block * step
        onehot = jnp.where(row == ids, 1.0, 0.0).astype(jnp.bfloat16)
        left = [logit_ref[span, s * LANES : (s + 1) * LANES] for s in spots]
        right = jnp.concatenate([c[:TOKENS, :] for c in chunks] + [c[TOKENS : TOKENS + SLOTS, :] for c in chunks], axis=0)
        total = jnp.dot(jnp.concatenate(left + [onehot], axis=1), right, preferred_element_type=jnp.float32)
        if added:
            total += refs[pieces][span, :]
        if others:
            over_ref, stage, sems = refs[pieces + added + others + 1 :]
            stage[span, :] = total
            copies.append(pltpu.make_async_copy(stage.at[span, :], out_ref.at[span, :], sems.at[block]))
            copies[-1].start()
        else:
            out_ref[span, :] = total
    if others:
        over = [c[TOKENS + SLOTS : TOKENS + SLOTS + CODES, :LANES] for c in chunks + refs[pieces + added :][:others]]
        over = functools.reduce(jnp.maximum, [c.astype(jnp.float32)[4:5] for c in over])
        over_ref[0] = jnp.max(over).astype(jnp.int32)
    for copy in copies:
        copy.wait()


def contract(offset, logits, chunks, spots, partial=None, others=()):
    rows, columns = logits.shape[0], chunks[0].shape[1]
    added = [] if partial is None else [partial]
    here = pl.BlockSpec(memory_space=pltpu.VMEM)
    out = jax.ShapeDtypeStruct((rows, columns), jnp.float32)
    scratch = [pltpu.VMEM((rows, columns), jnp.float32), pltpu.SemaphoreType.DMA((8,))]
    return pl.pallas_call(
        functools.partial(contract_kernel, tuple(spots), len(added), len(others)),
        out_shape=[out, jax.ShapeDtypeStruct((1,), jnp.int32)] if others else out,
        in_specs=[pl.BlockSpec(memory_space=pltpu.SMEM)] + [here] * (1 + len(chunks) + len(added) + len(others)),
        out_specs=[pl.BlockSpec(memory_space=pl.ANY), pl.BlockSpec(memory_space=pltpu.SMEM)] if others else here,
        scratch_shapes=scratch if others else [],
        compiler_params=pltpu.CompilerParams(vmem_limit_bytes=16 << 20),
        cost_estimate=pl.CostEstimate(
            flops=3 * rows * len(spots) * LANES * columns, bytes_accessed=8 << 20, transcendentals=0
        ),
    )(offset, logits, *chunks, *added, *others)


def append_kernel(pieces, slots, offset_ref, *refs):
    chunks, base_ref, out_ref = refs[:pieces], refs[pieces], refs[pieces + 1]
    rows = out_ref.shape[0]
    ids = slot_ids(chunks, 0, slots, offset_ref[0] + pl.program_id(0) * rows)
    row = lax.broadcasted_iota(jnp.int32, (rows, ids.shape[1]), 0)
    onehot = jnp.where(row == ids, 1.0, 0.0).astype(jnp.bfloat16)
    right = jnp.concatenate([c[:slots, :] for c in chunks], axis=0)
    out_ref[...] = base_ref[...] + jnp.dot(onehot, right, preferred_element_type=jnp.float32)


def append(offset, chunks, base):
    rows, columns = base.shape
    block = rows // 4
    whole = pl.BlockSpec(chunks[0].shape, lambda m: (0, 0), pipeline_mode=pl.Buffered(1))
    tile = pl.BlockSpec((block, columns), lambda m: (m, 0))
    return pl.pallas_call(
        functools.partial(append_kernel, len(chunks), chunks[0].shape[0] - CODES),
        out_shape=jax.ShapeDtypeStruct(base.shape, base.dtype),
        grid=(rows // block,),
        in_specs=[pl.BlockSpec(memory_space=pltpu.SMEM)] + [whole] * len(chunks) + [tile],
        out_specs=tile,
        input_output_aliases={1 + len(chunks): 0},
        compiler_params=pltpu.CompilerParams(vmem_limit_bytes=16 << 20),
    )(offset, *chunks, base)


def body(token_ids, hidden, logit_grad, embed_grad):
    dp, vocab = lax.axis_index("dp"), lax.axis_index("vocab")
    columns = hidden.shape[1] // 2
    offset = (vocab * logit_grad.shape[1]).astype(jnp.int32).reshape(1)
    ids = token_ids[:, None]
    lane = lax.broadcasted_iota(jnp.int32, (ROWS, LANES), 1)
    code = jnp.where(lane == 0, ids >> 9, jnp.where(lane == 1, (ids >> 1) & 255, ids & 1))
    code = jnp.where(lane < 3, code, 0).astype(jnp.bfloat16)

    def payload(side):
        pick = [lax.dynamic_slice_in_dim(a, side * columns, columns, 1) for a in (hidden, embed_grad)]
        return jnp.concatenate(pick + [code], axis=1)

    dims = (((0,), (0,)), ((), ()))
    token, away = arrangement(dp, vocab)
    z, _, yh, _ = coords(vocab)
    plane = jnp.stack([z, yh]).astype(jnp.int32)
    own, other, offset, token, plane = lax.optimization_barrier(
        (payload(dp), payload(1 - dp), offset, token, plane)
    )
    spot = lax.broadcasted_iota(jnp.int32, (logit_grad.shape[0], 1), 0)
    near, far = (((spot == token) & (away == side)).astype(jnp.bfloat16) for side in (0, 1))
    parts, early = gather_column(own, other)
    held, _ = lax.optimization_barrier((logit_grad, early))
    partner = move(held, fd=1)
    column, rest = pack(plane, parts, columns)
    swapped = move(column, fc=1)
    direct = move(column, dx=1)
    local, _ = lax.optimization_barrier((logit_grad, swapped))
    turned = lax.dot_general(local, near, dims, preferred_element_type=jnp.float32)
    turned = turned + lax.dot_general(partner, far, dims, preferred_element_type=jnp.float32)
    late, turned = lax.optimization_barrier((swapped, turned.astype(jnp.bfloat16)))
    passed = move(direct, dx=1)
    direct = [direct, move(late, dx=1)]
    first = [column, swapped] + direct
    partial = contract(offset, turned, first, (0, 1, 2, 3))
    passed, partial = lax.optimization_barrier((passed, partial))
    second = [passed] + [move(part, fc=1) for part in direct]
    partial = contract(offset, turned, second, (4, 5, 6), partial)
    result, over = contract(offset, turned, [move(passed, fc=1)], (7,), partial, first + second)

    def again(state):
        total, _ = state
        pair = [rest, move(rest, fc=1)]
        came = [move(part, dx=1) for part in pair]
        came.append(move(came[0], dx=1))
        return append(offset, pair + came + [move(part, fc=1) for part in came], total), jnp.int32(0)

    return lax.while_loop(lambda state: state[1] > 0, again, (result, over[0]))[0]


def solution(mesh):
    placed = (
        P(("dp", "vocab")),
        P(("dp", "vocab"), None),
        P("dp", "vocab"),
        P(("dp", "vocab"), None),
    )
    return jax.shard_map(
        body, mesh=mesh, in_specs=placed, out_specs=P("vocab", "dp"), check_vma=False
    )
```

```python
import functools

import jax
import jax.numpy as jnp
import numpy as np
from jax import lax
from jax.experimental import pallas as pl
from jax.experimental.pallas import tpu as pltpu
from jax.sharding import PartitionSpec as P

Z, X, YH, CORE, DP = 8, 4, 2, 2, 2
ROWS = 4
LANES = 128
TOKENS = 128
SLOTS = 32
CODES = 8


def coords(vocab):
    return vocab // (X * 4), (vocab // 4) % X, (vocab // 2) % 2, vocab % 2


def flat(dp, z, x, yh, core):
    return dp * (Z * X * 4) + ((z % Z) * X + (x % X)) * 4 + yh * 2 + core


def move(value, dz=0, dx=0, fy=0, fd=0, fc=0):
    pairs = []
    for dp in range(DP):
        for vocab in range(Z * X * 4):
            z, x, yh, core = coords(vocab)
            way = 1 - 2 * core
            pairs.append((flat(dp, z, x, yh, core), flat(dp ^ fd, z + way * dz, x + way * dx, yh ^ fy, core ^ fc)))
    return lax.ppermute(value, ("dp", "vocab"), pairs)


def gather_column(own, other):
    from_dy = move(other, fd=1, fy=1)
    from_dp = move(other, fd=1)
    from_yh = move(own, fy=1)
    chunk = jnp.concatenate([own, from_dp, from_yh, from_dy], axis=0)
    return chunk, move(chunk, fc=1), from_yh


def along_z(mine, both):
    two, one = move(both, dz=2), move(both, dz=1)
    three, four = move(two, dz=1), move(two[:16], dz=2)
    return [mine, one, two, three, four]


STEPS = (0, 0, 1, 1, 2, -1, -1, 2)
SWAPPED = (0, 1, 0, 1, 0, 1, 0, 1)


def arrangement(dp, vocab):
    z, x, yh, core = coords(vocab)
    place = lax.broadcasted_iota(jnp.int32, (1, 2 * Z * X * YH * CORE * ROWS), 1)
    j, r, part, column = place % 4, (place // 4) % 4, (place // 16) % Z, place // (16 * Z)
    steps, swapped = jnp.zeros_like(place), jnp.zeros_like(place)
    for k in range(len(STEPS)):
        steps = jnp.where(column == k, STEPS[k], steps)
        swapped = jnp.where(column == k, SWAPPED[k], swapped)
    way = 1 - 2 * core
    from_x = (x - way * steps + 2 * X) % X
    holder = core ^ swapped
    back = (part + 1) // 2
    from_z = (z - (1 - 2 * holder) * back + 2 * Z) % Z
    from_core = holder ^ jnp.where((part % 2 == 0) & (part > 0), 1, 0)
    token = ((from_z * X + from_x) * 2 + (yh ^ (r // 2))) * 2 + from_core
    return token * ROWS + j, r % 2


def pack_kernel(columns, plane_ref, *refs):
    parts, (out_ref, rest_ref) = refs[:-2], refs[-2:]
    side = (((1,), (1,)), ((), ()))
    grads = jnp.concatenate([p[:, :columns] for p in parts], axis=0)
    codes = jnp.concatenate([p[:, columns:] for p in parts], axis=0)
    line = lax.broadcasted_iota(jnp.int32, (2 * CODES, LANES), 0)
    lane = lax.broadcasted_iota(jnp.int32, (2 * CODES, LANES), 1)
    pick = jnp.where(line == lane, 1.0, 0.0).astype(jnp.bfloat16)
    turned = lax.dot_general(pick, codes, side, preferred_element_type=jnp.float32)
    top = turned[:1].astype(jnp.int32)
    match = ((top >> 5) == plane_ref[0]) & (((top >> 2) & 1) == plane_ref[1])
    found = jnp.where(match, 1.0, 0.0)
    row = lax.broadcasted_iota(jnp.int32, (TOKENS, TOKENS), 0)
    col = lax.broadcasted_iota(jnp.int32, (TOKENS, TOKENS), 1)
    before = jnp.where(row < col, 1.0, 0.0).astype(jnp.bfloat16)
    many = jnp.broadcast_to(found, (2 * CODES, TOKENS)).astype(jnp.bfloat16)
    rank = jnp.dot(many, before, preferred_element_type=jnp.float32)[:1].astype(jnp.int32)
    rank = jnp.where(match, rank, -1)
    over = jnp.max(jnp.where(rank >= SLOTS, 1.0, 0.0), axis=1, keepdims=True)
    turned = jnp.where(line == 3, 1.0, turned).astype(jnp.bfloat16)
    for ref, first, slots in ((out_ref, 0, SLOTS), (rest_ref, SLOTS, TOKENS - SLOTS)):
        chosen = jnp.where(rank == row[:slots] + first, 1.0, 0.0).astype(jnp.bfloat16)
        ref[:slots, :] = jnp.dot(chosen, grads, preferred_element_type=jnp.float32).astype(jnp.bfloat16)
        chosen = jnp.where(rank == row + first, 1.0, 0.0).astype(jnp.bfloat16)
        code = lax.dot_general(turned, chosen, side, preferred_element_type=jnp.float32)
        code = jnp.where(line == 4, over, code)[:CODES].astype(jnp.bfloat16)
        ref[slots : slots + CODES, :LANES] = code
        ref[slots : slots + CODES, LANES:] = jnp.zeros((CODES, columns - LANES), jnp.bfloat16)


def pack(plane, parts, columns):
    here = pl.BlockSpec(memory_space=pltpu.VMEM)
    shapes = (SLOTS + CODES, TOKENS - SLOTS + CODES)
    return pl.pallas_call(
        functools.partial(pack_kernel, columns),
        out_shape=[jax.ShapeDtypeStruct((rows, columns), jnp.bfloat16) for rows in shapes],
        in_specs=[pl.BlockSpec(memory_space=pltpu.SMEM)] + [here] * len(parts),
        out_specs=[here, here],
        compiler_params=pltpu.CompilerParams(vmem_limit_bytes=8 << 20),
        cost_estimate=pl.CostEstimate(flops=1 << 26, bytes_accessed=2 << 20, transcendentals=0),
    )(plane, *parts)


def blocks_of(packed, slots):
    size = slots + CODES
    return [p.at[k * size : (k + 1) * size, :] for p in packed for k in range(p.shape[0] // size)]


def slot_ids(packs, slots, offset):
    ids = []
    for c in packs:
        code = c[slots : slots + CODES, :LANES].astype(jnp.float32)
        row = (code[:1] * 512.0 + code[1:2] * 2.0 + code[2:3]).astype(jnp.int32) - offset
        ids.append(jnp.where(code[3:4] > 0.5, row, -1)[:, :slots])
    return jnp.concatenate(ids, axis=1)


def contract_kernel(spots, grads, added, others, offset_ref, logit_ref, *refs):
    pieces = len(spots)
    chunks, packs = refs[:pieces], blocks_of(refs[pieces : pieces + grads], SLOTS)
    rest = refs[pieces + grads :]
    out_ref = rest[added + others]
    rows = logit_ref.shape[0]
    blocks = 8 if others else 2
    step = rows // blocks
    ids = slot_ids(packs, SLOTS, offset_ref[0])
    copies = []
    for block in range(blocks):
        span = slice(block * step, (block + 1) * step)
        row = lax.broadcasted_iota(jnp.int32, (step, ids.shape[1]), 0) + block * step
        onehot = jnp.where(row == ids, 1.0, 0.0).astype(jnp.bfloat16)
        left = [logit_ref[span, s * LANES : (s + 1) * LANES] for s in spots]
        right = jnp.concatenate([c[...] for c in chunks] + [p[:SLOTS, :] for p in packs], axis=0)
        total = jnp.dot(jnp.concatenate(left + [onehot], axis=1), right, preferred_element_type=jnp.float32)
        if added:
            total += rest[0][span, :]
        if others:
            over_ref, stage, sems = rest[added + others + 1 :]
            stage[span, :] = total
            copies.append(pltpu.make_async_copy(stage.at[span, :], out_ref.at[span, :], sems.at[block]))
            copies[-1].start()
        else:
            out_ref[span, :] = total
    if others:
        over = [c[SLOTS : SLOTS + CODES, :LANES] for c in packs + blocks_of(rest[added : added + others], SLOTS)]
        over = functools.reduce(jnp.maximum, [c.astype(jnp.float32)[4:5] for c in over])
        over_ref[0] = jnp.max(over).astype(jnp.int32)
    for copy in copies:
        copy.wait()


def contract(offset, logits, chunks, spots, grads, partial=None, others=()):
    rows, columns = logits.shape[0], chunks[0].shape[1]
    added = [] if partial is None else [partial]
    here = pl.BlockSpec(memory_space=pltpu.VMEM)
    out = jax.ShapeDtypeStruct((rows, columns), jnp.float32)
    operands = [logits, *chunks, *grads, *added, *others]
    return pl.pallas_call(
        functools.partial(contract_kernel, tuple(spots), len(grads), len(added), len(others)),
        out_shape=[out, jax.ShapeDtypeStruct((1,), jnp.int32)] if others else out,
        in_specs=[pl.BlockSpec(memory_space=pltpu.SMEM)] + [here] * len(operands),
        out_specs=[pl.BlockSpec(memory_space=pl.ANY), pl.BlockSpec(memory_space=pltpu.SMEM)] if others else here,
        scratch_shapes=[pltpu.VMEM((rows, columns), jnp.float32), pltpu.SemaphoreType.DMA((8,))] if others else [],
        compiler_params=pltpu.CompilerParams(vmem_limit_bytes=16 << 20),
        cost_estimate=pl.CostEstimate(
            flops=3 * rows * len(spots) * LANES * columns, bytes_accessed=8 << 20, transcendentals=0
        ),
    )(offset, *operands)


def append_kernel(pieces, slots, offset_ref, *refs):
    chunks, base_ref, out_ref = refs[:pieces], refs[pieces], refs[pieces + 1]
    rows = out_ref.shape[0]
    ids = slot_ids(chunks, slots, offset_ref[0] + pl.program_id(0) * rows)
    row = lax.broadcasted_iota(jnp.int32, (rows, ids.shape[1]), 0)
    onehot = jnp.where(row == ids, 1.0, 0.0).astype(jnp.bfloat16)
    right = jnp.concatenate([c[:slots, :] for c in chunks], axis=0)
    out_ref[...] = base_ref[...] + jnp.dot(onehot, right, preferred_element_type=jnp.float32)


def append(offset, chunks, base):
    rows, columns = base.shape
    block = rows // 4
    whole = pl.BlockSpec(chunks[0].shape, lambda m: (0, 0), pipeline_mode=pl.Buffered(1))
    tile = pl.BlockSpec((block, columns), lambda m: (m, 0))
    return pl.pallas_call(
        functools.partial(append_kernel, len(chunks), chunks[0].shape[0] - CODES),
        out_shape=jax.ShapeDtypeStruct(base.shape, base.dtype),
        grid=(rows // block,),
        in_specs=[pl.BlockSpec(memory_space=pltpu.SMEM)] + [whole] * len(chunks) + [tile],
        out_specs=tile,
        input_output_aliases={1 + len(chunks): 0},
        compiler_params=pltpu.CompilerParams(vmem_limit_bytes=16 << 20),
    )(offset, *chunks, base)


def body(token_ids, hidden, logit_grad, embed_grad):
    dp, vocab = lax.axis_index("dp"), lax.axis_index("vocab")
    columns = hidden.shape[1] // 2
    offset = (vocab * logit_grad.shape[1]).astype(jnp.int32).reshape(1)
    ids = token_ids[:, None]
    lane = lax.broadcasted_iota(jnp.int32, (ROWS, LANES), 1)
    code = jnp.where(lane == 0, ids >> 9, jnp.where(lane == 1, (ids >> 1) & 255, ids & 1))
    code = jnp.where(lane < 3, code, 0).astype(jnp.bfloat16)

    def payload(side):
        pick = [lax.dynamic_slice_in_dim(a, side * columns, columns, 1) for a in (hidden, embed_grad)]
        return jnp.concatenate(pick + [code], axis=1)

    dims = (((0,), (0,)), ((), ()))
    token, away = arrangement(dp, vocab)
    z, _, yh, _ = coords(vocab)
    plane = jnp.stack([z, yh]).astype(jnp.int32)
    own, other, offset, token, plane = lax.optimization_barrier(
        (payload(dp), payload(1 - dp), offset, token, plane)
    )
    spot = lax.broadcasted_iota(jnp.int32, (logit_grad.shape[0], 1), 0)
    near, far = (((spot == token) & (away == side)).astype(jnp.bfloat16) for side in (0, 1))
    chunk, traded, early = gather_column(own, other)
    half = logit_grad.shape[0] // 2
    *held, _ = lax.optimization_barrier((logit_grad[:half], logit_grad[half:], early))
    partner = [move(held[0], fd=1)]
    mine = chunk[:, :columns], chunk[:, columns:]
    both = [jnp.concatenate(pair, axis=0) for pair in zip(mine, (traded[:, :columns], traded[:, columns:]))]
    hid, grads = along_z(mine[0], both[0]), along_z(mine[1], both[1])
    hid[4], grads[1], grads[2], partner[0] = lax.optimization_barrier((hid[4], grads[1], grads[2], partner[0]))
    column = jnp.concatenate(hid, axis=0)
    held[1], partner[0] = lax.optimization_barrier((held[1], partner[0]))
    partner.append(move(held[1], fd=1))
    swapped = move(column, fc=1)
    grads[0], swapped = lax.optimization_barrier((grads[0], swapped))
    packed, rest = pack(plane, grads, columns)
    direct = [move(column, dx=1), move(swapped, dx=1)]
    passed = move(direct[0], dx=1)
    pairs = [jnp.concatenate([packed, move(packed, fc=1)], axis=0)]
    pairs.append(move(pairs[0], dx=1))
    lone = move(pairs[1][: SLOTS + CODES], dx=1)
    local, partner[0], _ = lax.optimization_barrier((logit_grad, partner[0], swapped))
    turned = lax.dot_general(local, near, dims, preferred_element_type=jnp.float32)
    for part, spots in zip(partner, (far[:half], far[half:])):
        turned = turned + lax.dot_general(part, spots, dims, preferred_element_type=jnp.float32)
    *came, turned = lax.optimization_barrier((*direct, pairs[1], turned.astype(jnp.bfloat16)))
    partial = contract(offset, turned, [column, swapped] + direct, (0, 1, 2, 3), pairs[:1])
    passed, lone, partial = lax.optimization_barrier((passed, lone, partial))
    came = [move(part, fc=1) for part in came]
    pairs.append(came.pop())
    partial = contract(offset, turned, [passed] + came, (4, 5, 6), pairs[1:], partial)
    lone = [lone, move(lone, fc=1)]
    result, over = contract(offset, turned, [move(passed, fc=1)], (7,), lone, partial, pairs)

    def again(state):
        total, _ = state
        pair = [rest, move(rest, fc=1)]
        came = [move(part, dx=1) for part in pair]
        came.append(move(came[0], dx=1))
        return append(offset, pair + came + [move(part, fc=1) for part in came], total), jnp.int32(0)

    return lax.while_loop(lambda state: state[1] > 0, again, (result, over[0]))[0]


def solution(mesh):
    placed = (
        P(("dp", "vocab")),
        P(("dp", "vocab"), None),
        P("dp", "vocab"),
        P(("dp", "vocab"), None),
    )
    return jax.shard_map(
        body, mesh=mesh, in_specs=placed, out_specs=P("vocab", "dp"), check_vma=False
    )
```

```python
import functools

import jax
import jax.numpy as jnp
import numpy as np
from jax import lax
from jax.experimental import pallas as pl
from jax.experimental.pallas import tpu as pltpu
from jax.sharding import PartitionSpec as P

Z, X, YH, CORE, DP = 8, 4, 2, 2, 2
ROWS = 4
LANES = 128
TOKENS = 128
SLOTS = 32
CODES = 8


def coords(vocab):
    return vocab // (X * 4), (vocab // 4) % X, (vocab // 2) % 2, vocab % 2


def flat(dp, z, x, yh, core):
    return dp * (Z * X * 4) + ((z % Z) * X + (x % X)) * 4 + yh * 2 + core


def move(value, dz=0, dx=0, fy=0, fd=0, fc=0):
    pairs = []
    for dp in range(DP):
        for vocab in range(Z * X * 4):
            z, x, yh, core = coords(vocab)
            way = 1 - 2 * core
            pairs.append((flat(dp, z, x, yh, core), flat(dp ^ fd, z + way * dz, x + way * dx, yh ^ fy, core ^ fc)))
    return lax.ppermute(value, ("dp", "vocab"), pairs)


def gather_column(own, other):
    from_dy = move(other, fd=1, fy=1)
    from_dp = move(other, fd=1)
    from_yh = move(own, fy=1)
    chunk = jnp.concatenate([own, from_dp, from_yh, from_dy], axis=0)
    both = jnp.concatenate([chunk, move(chunk, fc=1)], axis=0)
    two, one = move(both, dz=2), move(both, dz=1)
    three, four = move(two, dz=1), move(two[:16], dz=2)
    return [chunk, one, two, three, four], from_yh


STEPS = (0, 0, 1, 1, 2, -1, -1, 2)
SWAPPED = (0, 1, 0, 1, 0, 1, 0, 1)


def arrangement(dp, vocab):
    z, x, yh, core = coords(vocab)
    place = lax.broadcasted_iota(jnp.int32, (1, 2 * Z * X * YH * CORE * ROWS), 1)
    j, r, part, column = place % 4, (place // 4) % 4, (place // 16) % Z, place // (16 * Z)
    steps, swapped = jnp.zeros_like(place), jnp.zeros_like(place)
    for k in range(len(STEPS)):
        steps = jnp.where(column == k, STEPS[k], steps)
        swapped = jnp.where(column == k, SWAPPED[k], swapped)
    way = 1 - 2 * core
    from_x = (x - way * steps + 2 * X) % X
    holder = core ^ swapped
    back = (part + 1) // 2
    from_z = (z - (1 - 2 * holder) * back + 2 * Z) % Z
    from_core = holder ^ jnp.where((part % 2 == 0) & (part > 0), 1, 0)
    token = ((from_z * X + from_x) * 2 + (yh ^ (r // 2))) * 2 + from_core
    return token * ROWS + j, r % 2


def pack_kernel(columns, start, first, slots, plane_ref, *refs):
    parts, ref = refs[:-1], refs[-1]
    side = (((1,), (1,)), ((), ()))
    if start:
        ref[:start, :] = jnp.concatenate([p[:, :columns] for p in parts], axis=0)
    grads = jnp.concatenate([p[:, columns : 2 * columns] for p in parts], axis=0)
    codes = jnp.concatenate([p[:, 2 * columns :] for p in parts], axis=0)
    line = lax.broadcasted_iota(jnp.int32, (CODES, LANES), 0)
    lane = lax.broadcasted_iota(jnp.int32, (CODES, LANES), 1)
    pick = jnp.where(line == lane, 1.0, 0.0).astype(jnp.bfloat16)
    turned = lax.dot_general(pick, codes, side, preferred_element_type=jnp.float32)
    top = turned[:1].astype(jnp.int32)
    match = ((top >> 5) == plane_ref[0]) & (((top >> 2) & 1) == plane_ref[1])
    found = jnp.where(match, 1.0, 0.0)
    row = lax.broadcasted_iota(jnp.int32, (TOKENS, TOKENS), 0)
    col = lax.broadcasted_iota(jnp.int32, (TOKENS, TOKENS), 1)
    before = jnp.where(row < col, 1.0, 0.0).astype(jnp.bfloat16)
    many = jnp.broadcast_to(found, (CODES, TOKENS)).astype(jnp.bfloat16)
    rank = jnp.dot(many, before, preferred_element_type=jnp.float32)[:1].astype(jnp.int32)
    rank = jnp.where(match, rank, -1)
    over = jnp.max(jnp.where(rank >= SLOTS, 1.0, 0.0), axis=1, keepdims=True)
    turned = jnp.where(line == 3, 1.0, turned).astype(jnp.bfloat16)
    chosen = jnp.where(rank == row[:slots] + first, 1.0, 0.0).astype(jnp.bfloat16)
    ref[start : start + slots, :] = jnp.dot(chosen, grads, preferred_element_type=jnp.float32).astype(jnp.bfloat16)
    chosen = jnp.where(rank == row + first, 1.0, 0.0).astype(jnp.bfloat16)
    code = lax.dot_general(turned, chosen, side, preferred_element_type=jnp.float32)
    code = jnp.where(line == 4, over, code).astype(jnp.bfloat16)
    ref[start + slots : start + slots + CODES, :LANES] = code
    ref[start + slots : start + slots + CODES, LANES:] = jnp.zeros((CODES, columns - LANES), jnp.bfloat16)


def pack(plane, parts, columns, start, first, slots):
    here = pl.BlockSpec(memory_space=pltpu.VMEM)
    return pl.pallas_call(
        functools.partial(pack_kernel, columns, start, first, slots),
        out_shape=jax.ShapeDtypeStruct((start + slots + CODES, columns), jnp.bfloat16),
        in_specs=[pl.BlockSpec(memory_space=pltpu.SMEM)] + [here] * len(parts),
        out_specs=here,
        compiler_params=pltpu.CompilerParams(vmem_limit_bytes=8 << 20),
        cost_estimate=pl.CostEstimate(flops=1 << 26, bytes_accessed=2 << 20, transcendentals=0),
    )(plane, *parts)


def slot_ids(chunks, first, slots, offset):
    ids = []
    for c in chunks:
        code = c[first + slots : first + slots + CODES, :LANES].astype(jnp.float32)
        row = (code[:1] * 512.0 + code[1:2] * 2.0 + code[2:3]).astype(jnp.int32) - offset
        ids.append(jnp.where(code[3:4] > 0.5, row, -1)[:, :slots])
    return jnp.concatenate(ids, axis=1)


def contract_kernel(spots, added, others, offset_ref, logit_ref, *refs):
    pieces = len(spots)
    chunks = refs[:pieces]
    out_ref = refs[pieces + added + others]
    rows = logit_ref.shape[0]
    blocks = 8 if others else 2
    step = rows // blocks
    ids = slot_ids(chunks, TOKENS, SLOTS, offset_ref[0])
    copies = []
    for block in range(blocks):
        span = slice(block * step, (block + 1) * step)
        row = lax.broadcasted_iota(jnp.int32, (step, ids.shape[1]), 0) + block * step
        onehot = jnp.where(row == ids, 1.0, 0.0).astype(jnp.bfloat16)
        left = [logit_ref[span, s * LANES : (s + 1) * LANES] for s in spots]
        right = jnp.concatenate([c[:TOKENS, :] for c in chunks] + [c[TOKENS : TOKENS + SLOTS, :] for c in chunks], axis=0)
        total = jnp.dot(jnp.concatenate(left + [onehot], axis=1), right, preferred_element_type=jnp.float32)
        if added:
            total += refs[pieces][span, :]
        if others:
            over_ref, stage, sems = refs[pieces + added + others + 1 :]
            stage[span, :] = total
            copies.append(pltpu.make_async_copy(stage.at[span, :], out_ref.at[span, :], sems.at[block]))
            copies[-1].start()
        else:
            out_ref[span, :] = total
    if others:
        over = [c[TOKENS + SLOTS : TOKENS + SLOTS + CODES, :LANES] for c in chunks + refs[pieces + added :][:others]]
        over = functools.reduce(jnp.maximum, [c.astype(jnp.float32)[4:5] for c in over])
        over_ref[0] = jnp.max(over).astype(jnp.int32)
    for copy in copies:
        copy.wait()


def contract(offset, logits, chunks, spots, partial=None, others=()):
    rows, columns = logits.shape[0], chunks[0].shape[1]
    added = [] if partial is None else [partial]
    here = pl.BlockSpec(memory_space=pltpu.VMEM)
    out = jax.ShapeDtypeStruct((rows, columns), jnp.float32)
    scratch = [pltpu.VMEM((rows, columns), jnp.float32), pltpu.SemaphoreType.DMA((8,))]
    return pl.pallas_call(
        functools.partial(contract_kernel, tuple(spots), len(added), len(others)),
        out_shape=[out, jax.ShapeDtypeStruct((1,), jnp.int32)] if others else out,
        in_specs=[pl.BlockSpec(memory_space=pltpu.SMEM)] + [here] * (1 + len(chunks) + len(added) + len(others)),
        out_specs=[pl.BlockSpec(memory_space=pl.ANY), pl.BlockSpec(memory_space=pltpu.SMEM)] if others else here,
        scratch_shapes=scratch if others else [],
        compiler_params=pltpu.CompilerParams(vmem_limit_bytes=16 << 20),
        cost_estimate=pl.CostEstimate(
            flops=3 * rows * len(spots) * LANES * columns, bytes_accessed=8 << 20, transcendentals=0
        ),
    )(offset, logits, *chunks, *added, *others)


def append_kernel(pieces, slots, offset_ref, *refs):
    chunks, base_ref, out_ref = refs[:pieces], refs[pieces], refs[pieces + 1]
    rows = out_ref.shape[0]
    ids = slot_ids(chunks, 0, slots, offset_ref[0] + pl.program_id(0) * rows)
    row = lax.broadcasted_iota(jnp.int32, (rows, ids.shape[1]), 0)
    onehot = jnp.where(row == ids, 1.0, 0.0).astype(jnp.bfloat16)
    right = jnp.concatenate([c[:slots, :] for c in chunks], axis=0)
    out_ref[...] = base_ref[...] + jnp.dot(onehot, right, preferred_element_type=jnp.float32)


def append(offset, chunks, base):
    rows, columns = base.shape
    block = rows // 4
    whole = pl.BlockSpec(chunks[0].shape, lambda m: (0, 0), pipeline_mode=pl.Buffered(1))
    tile = pl.BlockSpec((block, columns), lambda m: (m, 0))
    return pl.pallas_call(
        functools.partial(append_kernel, len(chunks), chunks[0].shape[0] - CODES),
        out_shape=jax.ShapeDtypeStruct(base.shape, base.dtype),
        grid=(rows // block,),
        in_specs=[pl.BlockSpec(memory_space=pltpu.SMEM)] + [whole] * len(chunks) + [tile],
        out_specs=tile,
        input_output_aliases={1 + len(chunks): 0},
        compiler_params=pltpu.CompilerParams(vmem_limit_bytes=16 << 20),
    )(offset, *chunks, base)


def body(token_ids, hidden, logit_grad, embed_grad):
    dp, vocab = lax.axis_index("dp"), lax.axis_index("vocab")
    columns = hidden.shape[1] // 2
    offset = (vocab * logit_grad.shape[1]).astype(jnp.int32).reshape(1)
    ids = token_ids[:, None]
    lane = lax.broadcasted_iota(jnp.int32, (ROWS, LANES), 1)
    code = jnp.where(lane == 0, ids >> 9, jnp.where(lane == 1, (ids >> 1) & 255, ids & 1))
    code = jnp.where(lane < 3, code, 0).astype(jnp.bfloat16)

    def payload(side):
        pick = [lax.dynamic_slice_in_dim(a, side * columns, columns, 1) for a in (hidden, embed_grad)]
        return jnp.concatenate(pick + [code], axis=1)

    dims = (((0,), (0,)), ((), ()))
    token, away = arrangement(dp, vocab)
    z, _, yh, _ = coords(vocab)
    plane = jnp.stack([z, yh]).astype(jnp.int32)
    own, other, offset, token, plane = lax.optimization_barrier(
        (payload(dp), payload(1 - dp), offset, token, plane)
    )
    spot = lax.broadcasted_iota(jnp.int32, (logit_grad.shape[0], 1), 0)
    near, far = (((spot == token) & (away == side)).astype(jnp.bfloat16) for side in (0, 1))
    parts, early = gather_column(own, other)
    held, _ = lax.optimization_barrier((logit_grad, early))
    partner = move(held, fd=1)
    column = pack(plane, parts, columns, TOKENS, 0, SLOTS)
    swapped = move(column, fc=1)
    direct = [move(column, dx=1), move(swapped, dx=1)]
    local, _ = lax.optimization_barrier((logit_grad, swapped))
    turned = lax.dot_general(local, near, dims, preferred_element_type=jnp.float32)
    turned = turned + lax.dot_general(partner, far, dims, preferred_element_type=jnp.float32)
    passed = move(direct[0], dx=1)
    came, turned = lax.optimization_barrier((direct[0], turned.astype(jnp.bfloat16)))
    first = [column, swapped] + direct
    partial = contract(offset, turned, first, (0, 1, 2, 3))
    *parts, partial = lax.optimization_barrier((*parts, partial))
    rest = pack(plane, parts, columns, 0, SLOTS, TOKENS - SLOTS)
    passed, partial, rest = lax.optimization_barrier((passed, partial, rest))
    second = [passed] + [move(part, fc=1) for part in (came, direct[1])]
    partial = contract(offset, turned, second, (4, 5, 6), partial)
    result, over = contract(offset, turned, [move(passed, fc=1)], (7,), partial, first + second)

    def again(state):
        total, _ = state
        pair = [rest, move(rest, fc=1)]
        came = [move(part, dx=1) for part in pair]
        came.append(move(came[0], dx=1))
        return append(offset, pair + came + [move(part, fc=1) for part in came], total), jnp.int32(0)

    return lax.while_loop(lambda state: state[1] > 0, again, (result, over[0]))[0]


def solution(mesh):
    placed = (
        P(("dp", "vocab")),
        P(("dp", "vocab"), None),
        P("dp", "vocab"),
        P(("dp", "vocab"), None),
    )
    return jax.shard_map(
        body, mesh=mesh, in_specs=placed, out_specs=P("vocab", "dp"), check_vma=False
    )
```

```python
import functools

import jax
import jax.numpy as jnp
import numpy as np
from jax import lax
from jax.experimental import pallas as pl
from jax.experimental.pallas import tpu as pltpu
from jax.sharding import PartitionSpec as P

Z, X, YH, CORE, DP = 8, 4, 2, 2, 2
ROWS = 4
LANES = 128
TOKENS = 128
SLOTS = 32
CODES = 8


def coords(vocab):
    return vocab // (X * 4), (vocab // 4) % X, (vocab // 2) % 2, vocab % 2


def flat(dp, z, x, yh, core):
    return dp * (Z * X * 4) + ((z % Z) * X + (x % X)) * 4 + yh * 2 + core


def move(value, dz=0, dx=0, fy=0, fd=0, fc=0):
    pairs = []
    for dp in range(DP):
        for vocab in range(Z * X * 4):
            z, x, yh, core = coords(vocab)
            way = 1 - 2 * core
            pairs.append((flat(dp, z, x, yh, core), flat(dp ^ fd, z + way * dz, x + way * dx, yh ^ fy, core ^ fc)))
    return lax.ppermute(value, ("dp", "vocab"), pairs)


def gather_column(own, other):
    from_dy = move(other, fd=1, fy=1)
    from_dp = move(other, fd=1)
    from_yh = move(own, fy=1)
    chunk = jnp.concatenate([own, from_dp, from_yh, from_dy], axis=0)
    both = jnp.concatenate([chunk, move(chunk, fc=1)], axis=0)
    two, one = move(both, dz=2), move(both, dz=1)
    three, four = move(two, dz=1), move(two[:16], dz=2)
    return [chunk, one, two, three, four]


STEPS = (0, 0, 1, 1, 2, -1, -1, 2)
SWAPPED = (0, 1, 0, 1, 0, 1, 0, 1)


def arrangement(dp, vocab):
    z, x, yh, core = coords(vocab)
    place = lax.broadcasted_iota(jnp.int32, (1, 2 * Z * X * YH * CORE * ROWS), 1)
    j, r, part, column = place % 4, (place // 4) % 4, (place // 16) % Z, place // (16 * Z)
    steps, swapped = jnp.zeros_like(place), jnp.zeros_like(place)
    for k in range(len(STEPS)):
        steps = jnp.where(column == k, STEPS[k], steps)
        swapped = jnp.where(column == k, SWAPPED[k], swapped)
    way = 1 - 2 * core
    from_x = (x - way * steps + 2 * X) % X
    holder = core ^ swapped
    back = (part + 1) // 2
    from_z = (z - (1 - 2 * holder) * back + 2 * Z) % Z
    from_core = holder ^ jnp.where((part % 2 == 0) & (part > 0), 1, 0)
    token = ((from_z * X + from_x) * 2 + (yh ^ (r // 2))) * 2 + from_core
    return token * ROWS + j, r % 2


def pack_kernel(columns, start, first, slots, plane_ref, *refs):
    parts, ref = refs[:-1], refs[-1]
    side = (((1,), (1,)), ((), ()))
    if start:
        ref[:start, :] = jnp.concatenate([p[:, :columns] for p in parts], axis=0)
    grads = jnp.concatenate([p[:, columns : 2 * columns] for p in parts], axis=0)
    codes = jnp.concatenate([p[:, 2 * columns :] for p in parts], axis=0)
    line = lax.broadcasted_iota(jnp.int32, (CODES, LANES), 0)
    lane = lax.broadcasted_iota(jnp.int32, (CODES, LANES), 1)
    pick = jnp.where(line == lane, 1.0, 0.0).astype(jnp.bfloat16)
    turned = lax.dot_general(pick, codes, side, preferred_element_type=jnp.float32)
    top = turned[:1].astype(jnp.int32)
    match = ((top >> 5) == plane_ref[0]) & (((top >> 2) & 1) == plane_ref[1])
    found = jnp.where(match, 1.0, 0.0)
    row = lax.broadcasted_iota(jnp.int32, (TOKENS, TOKENS), 0)
    col = lax.broadcasted_iota(jnp.int32, (TOKENS, TOKENS), 1)
    before = jnp.where(row < col, 1.0, 0.0).astype(jnp.bfloat16)
    many = jnp.broadcast_to(found, (CODES, TOKENS)).astype(jnp.bfloat16)
    rank = jnp.dot(many, before, preferred_element_type=jnp.float32)[:1].astype(jnp.int32)
    rank = jnp.where(match, rank, -1)
    over = jnp.max(jnp.where(rank >= SLOTS, 1.0, 0.0), axis=1, keepdims=True)
    turned = jnp.where(line == 3, 1.0, turned).astype(jnp.bfloat16)
    chosen = jnp.where(rank == row[:slots] + first, 1.0, 0.0).astype(jnp.bfloat16)
    ref[start : start + slots, :] = jnp.dot(chosen, grads, preferred_element_type=jnp.float32).astype(jnp.bfloat16)
    chosen = jnp.where(rank == row + first, 1.0, 0.0).astype(jnp.bfloat16)
    code = lax.dot_general(turned, chosen, side, preferred_element_type=jnp.float32)
    code = jnp.where(line == 4, over, code).astype(jnp.bfloat16)
    ref[start + slots : start + slots + CODES, :LANES] = code
    ref[start + slots : start + slots + CODES, LANES:] = jnp.zeros((CODES, columns - LANES), jnp.bfloat16)


def pack(plane, parts, columns, start, first, slots):
    here = pl.BlockSpec(memory_space=pltpu.VMEM)
    return pl.pallas_call(
        functools.partial(pack_kernel, columns, start, first, slots),
        out_shape=jax.ShapeDtypeStruct((start + slots + CODES, columns), jnp.bfloat16),
        in_specs=[pl.BlockSpec(memory_space=pltpu.SMEM)] + [here] * len(parts),
        out_specs=here,
        compiler_params=pltpu.CompilerParams(vmem_limit_bytes=8 << 20),
        cost_estimate=pl.CostEstimate(flops=1 << 26, bytes_accessed=2 << 20, transcendentals=0),
    )(plane, *parts)


def slot_ids(chunks, first, slots, offset):
    ids = []
    for c in chunks:
        code = c[first + slots : first + slots + CODES, :LANES].astype(jnp.float32)
        row = (code[:1] * 512.0 + code[1:2] * 2.0 + code[2:3]).astype(jnp.int32) - offset
        ids.append(jnp.where(code[3:4] > 0.5, row, -1)[:, :slots])
    return jnp.concatenate(ids, axis=1)


def contract_kernel(spots, added, others, offset_ref, logit_ref, *refs):
    pieces = len(spots)
    chunks = refs[:pieces]
    out_ref = refs[pieces + added + others]
    rows = logit_ref.shape[0]
    blocks = 8 if others else 2
    step = rows // blocks
    ids = slot_ids(chunks, TOKENS, SLOTS, offset_ref[0])
    copies = []
    for block in range(blocks):
        span = slice(block * step, (block + 1) * step)
        row = lax.broadcasted_iota(jnp.int32, (step, ids.shape[1]), 0) + block * step
        onehot = jnp.where(row == ids, 1.0, 0.0).astype(jnp.bfloat16)
        left = [logit_ref[span, s * LANES : (s + 1) * LANES] for s in spots]
        right = jnp.concatenate([c[:TOKENS, :] for c in chunks] + [c[TOKENS : TOKENS + SLOTS, :] for c in chunks], axis=0)
        total = jnp.dot(jnp.concatenate(left + [onehot], axis=1), right, preferred_element_type=jnp.float32)
        if added:
            total += refs[pieces][span, :]
        if others:
            over_ref, stage, sems = refs[pieces + added + others + 1 :]
            stage[span, :] = total
            copies.append(pltpu.make_async_copy(stage.at[span, :], out_ref.at[span, :], sems.at[block]))
            copies[-1].start()
        else:
            out_ref[span, :] = total
    if others:
        over = [c[TOKENS + SLOTS : TOKENS + SLOTS + CODES, :LANES] for c in chunks + refs[pieces + added :][:others]]
        over = functools.reduce(jnp.maximum, [c.astype(jnp.float32)[4:5] for c in over])
        over_ref[0] = jnp.max(over).astype(jnp.int32)
    for copy in copies:
        copy.wait()


def contract(offset, logits, chunks, spots, partial=None, others=()):
    rows, columns = logits.shape[0], chunks[0].shape[1]
    added = [] if partial is None else [partial]
    here = pl.BlockSpec(memory_space=pltpu.VMEM)
    out = jax.ShapeDtypeStruct((rows, columns), jnp.float32)
    scratch = [pltpu.VMEM((rows, columns), jnp.float32), pltpu.SemaphoreType.DMA((8,))]
    return pl.pallas_call(
        functools.partial(contract_kernel, tuple(spots), len(added), len(others)),
        out_shape=[out, jax.ShapeDtypeStruct((1,), jnp.int32)] if others else out,
        in_specs=[pl.BlockSpec(memory_space=pltpu.SMEM)] + [here] * (1 + len(chunks) + len(added) + len(others)),
        out_specs=[pl.BlockSpec(memory_space=pl.ANY), pl.BlockSpec(memory_space=pltpu.SMEM)] if others else here,
        scratch_shapes=scratch if others else [],
        compiler_params=pltpu.CompilerParams(vmem_limit_bytes=16 << 20),
        cost_estimate=pl.CostEstimate(
            flops=3 * rows * len(spots) * LANES * columns, bytes_accessed=8 << 20, transcendentals=0
        ),
    )(offset, logits, *chunks, *added, *others)


def append_kernel(pieces, slots, offset_ref, *refs):
    chunks, base_ref, out_ref = refs[:pieces], refs[pieces], refs[pieces + 1]
    rows = out_ref.shape[0]
    ids = slot_ids(chunks, 0, slots, offset_ref[0] + pl.program_id(0) * rows)
    row = lax.broadcasted_iota(jnp.int32, (rows, ids.shape[1]), 0)
    onehot = jnp.where(row == ids, 1.0, 0.0).astype(jnp.bfloat16)
    right = jnp.concatenate([c[:slots, :] for c in chunks], axis=0)
    out_ref[...] = base_ref[...] + jnp.dot(onehot, right, preferred_element_type=jnp.float32)


def append(offset, chunks, base):
    rows, columns = base.shape
    block = rows // 4
    whole = pl.BlockSpec(chunks[0].shape, lambda m: (0, 0), pipeline_mode=pl.Buffered(1))
    tile = pl.BlockSpec((block, columns), lambda m: (m, 0))
    return pl.pallas_call(
        functools.partial(append_kernel, len(chunks), chunks[0].shape[0] - CODES),
        out_shape=jax.ShapeDtypeStruct(base.shape, base.dtype),
        grid=(rows // block,),
        in_specs=[pl.BlockSpec(memory_space=pltpu.SMEM)] + [whole] * len(chunks) + [tile],
        out_specs=tile,
        input_output_aliases={1 + len(chunks): 0},
        compiler_params=pltpu.CompilerParams(vmem_limit_bytes=16 << 20),
    )(offset, *chunks, base)


def body(token_ids, hidden, logit_grad, embed_grad):
    dp, vocab = lax.axis_index("dp"), lax.axis_index("vocab")
    columns = hidden.shape[1] // 2
    offset = (vocab * logit_grad.shape[1]).astype(jnp.int32).reshape(1)
    ids = token_ids[:, None]
    lane = lax.broadcasted_iota(jnp.int32, (ROWS, LANES), 1)
    code = jnp.where(lane == 0, ids >> 9, jnp.where(lane == 1, (ids >> 1) & 255, ids & 1))
    code = jnp.where(lane < 3, code, 0).astype(jnp.bfloat16)

    def payload(side):
        pick = [lax.dynamic_slice_in_dim(a, side * columns, columns, 1) for a in (hidden, embed_grad)]
        return jnp.concatenate(pick + [code], axis=1)

    dims = (((0,), (0,)), ((), ()))
    token, away = arrangement(dp, vocab)
    z, _, yh, _ = coords(vocab)
    plane = jnp.stack([z, yh]).astype(jnp.int32)
    own, other, offset, token, plane = lax.optimization_barrier(
        (payload(dp), payload(1 - dp), offset, token, plane)
    )
    spot = lax.broadcasted_iota(jnp.int32, (logit_grad.shape[0], 1), 0)
    near, far = (((spot == token) & (away == side)).astype(jnp.bfloat16) for side in (0, 1))
    parts = gather_column(own, other)
    partner = move(logit_grad, fd=1)
    column = pack(plane, parts, columns, TOKENS, 0, SLOTS)
    swapped = move(column, fc=1)
    direct = [move(column, dx=1), move(swapped, dx=1)]
    local, _ = lax.optimization_barrier((logit_grad, swapped))
    turned = lax.dot_general(local, near, dims, preferred_element_type=jnp.float32)
    turned = turned + lax.dot_general(partner, far, dims, preferred_element_type=jnp.float32)
    passed = move(direct[0], dx=1)
    came, turned = lax.optimization_barrier((direct[0], turned.astype(jnp.bfloat16)))
    first = [column, swapped] + direct
    partial = contract(offset, turned, first, (0, 1, 2, 3))
    *parts, partial = lax.optimization_barrier((*parts, partial))
    rest = pack(plane, parts, columns, 0, SLOTS, TOKENS - SLOTS)
    passed, partial, rest = lax.optimization_barrier((passed, partial, rest))
    second = [passed] + [move(part, fc=1) for part in (came, direct[1])]
    partial = contract(offset, turned, second, (4, 5, 6), partial)
    result, over = contract(offset, turned, [move(passed, fc=1)], (7,), partial, first + second)

    def again(state):
        total, _ = state
        pair = [rest, move(rest, fc=1)]
        came = [move(part, dx=1) for part in pair]
        came.append(move(came[0], dx=1))
        return append(offset, pair + came + [move(part, fc=1) for part in came], total), jnp.int32(0)

    return lax.while_loop(lambda state: state[1] > 0, again, (result, over[0]))[0]


def solution(mesh):
    placed = (
        P(("dp", "vocab")),
        P(("dp", "vocab"), None),
        P("dp", "vocab"),
        P(("dp", "vocab"), None),
    )
    return jax.shard_map(
        body, mesh=mesh, in_specs=placed, out_specs=P("vocab", "dp"), check_vma=False
    )
```
